32 devices in a mesh: groups: 2 (over y), ctx: 8 (over z, x), head: 2 (over core).
Axes of the slice: x: 2, y: 2, z: 4, core: 2. Of those that a mesh axis runs over, the one named last changes fastest.
Arguments:
- queries: bfloat16 [2048, 2048], P(('groups', 'ctx'), 'head'), parts along dimension 0, may hold values from -16 to 16
- key_states: bfloat16 [2048, 1024], P(('groups', 'ctx'), 'head'), parts along dimension 0, may hold values from -16 to 16
- value_states: bfloat16 [2048, 1024], P(('groups', 'ctx'), 'head'), parts along dimension 0, may hold values from -6 to 6
- out_grad: bfloat16 [2048, 2048], P(('groups', 'ctx'), 'head'), parts along dimension 0, may hold values from -6 to 6
- doc_ids: int32 [32], P('groups'), parts along dimension 0, may hold values from 0 to 5, never falling along the last dimension, each value on 1 to 8 neighbouring positions
- int_pos: int32 [128], P('groups'), parts along dimension 0, may hold values from 0 to 127, as said below
- hidden: bfloat16 [128, 4608], P('groups', 'ctx'), parts along dimension 0, may hold values from -6 to 6
- upstream: bfloat16 [128, 4608], P('groups', 'ctx'), parts along dimension 0, may hold values from -3 to 3
- w_query: bfloat16 [4608, 2048], P('ctx', 'head'), may hold values from -0.09375 to 0.09375
- w_key: bfloat16 [4608, 1024], P('ctx', 'head'), may hold values from -0.09375 to 0.09375
- w_value: bfloat16 [4608, 1024], P('ctx', 'head'), may hold values from -0.09375 to 0.09375
- rotation: float32 [8, 4608], P(None, 'ctx'), may hold values from -0.09375 to 0.09375
- projection: float32 [8, 4608], P(None, 'ctx'), may hold values from -0.09375 to 0.09375
- rank_bias: float32 [8], replicated, may hold values from -4 to 4
Outputs:
- grad_rot: float32 [16, 4608], P('groups', 'ctx'), parts along dimension 0
- grad_proj: float32 [16, 4608], P('groups', 'ctx'), parts along dimension 0
- grad_bias: float32 [16], P('groups'), parts along dimension 0
The draws below stay inside these ranges and needn't reach their ends.
There are 2 independent parts, one for each index of `groups`. The reference program is written for one: setup_inputs(seed, part) draws one part's arguments, and reference() takes and returns one part's arrays. A program takes and returns all parts, laid end to end along the dimension named above; an argument that names none is the same for every part. Nothing has to cross between parts.
Inputs may be any that keep to these rules, and one draw needn't show every extreme that they name: `doc_ids`: ids never fall along the blocks; each document covers 1 to 8 consecutive blocks, and one covers exactly 8. `int_pos`: each aligned group of 8 entries belongs to one block of 128 tokens and holds distinct token indices inside that block in rising order.
All inputs are finite; a program needn't handle non-finite values.
Results may differ from the reference program's by a relative error of at most 0.004.
The reference program's roundings to bfloat16 on the way count: a program that leaves them out, or rounds other values in their place, can miss the bound.
Values may be sent and summed in bfloat16 or wider, within the bound.
A program may use at most 64 MiB of HBM per device.

```python
import math
import jax
import jax.numpy as jnp
import numpy as np
from jax import lax

D = 4608
QH = 16
KVH = 8
HD = 128
RANK = 8
BLK = 64
POS_DEV = 8
DOCS = 6
TOK_DEV = 128
CTXLEN = 1024
NBLK = 16
DOC_MOST = 8
POS_ALL = 64


def draw_int_pos(key, part):
    block_count = POS_ALL // POS_DEV
    block_keys = jax.random.split(jax.random.fold_in(key, 11), block_count)

    def draw_block(block_key):
        shuffled = jax.random.permutation(block_key, TOK_DEV)
        return jnp.sort(shuffled[:POS_DEV]).astype(jnp.int32)
    return jax.vmap(draw_block)(block_keys).reshape(POS_ALL)


def scaled_rows(key, head_count, salt):
    salted = jax.random.fold_in(key, salt)
    base_key, scale_key = jax.random.split(salted)
    base_vals = jax.random.truncated_normal(base_key, -4.0, 4.0, (CTXLEN, head_count, HD), jnp.float32)
    top_scale = 4.0
    row_scale = jnp.exp(jax.random.uniform(scale_key, (CTXLEN, head_count, 1), jnp.float32, 0.0, math.log(top_scale)))
    return (base_vals * row_scale).reshape(CTXLEN, head_count * HD).astype(jnp.bfloat16)


def draw_queries(key, part):
    return scaled_rows(key, QH, 21)


def draw_key_states(key, part):
    return scaled_rows(key, KVH, 22)


def block_scale(stream_key, extent, shards, smallest, high):
    factor_of = 1.0
    for position, parts in shards:
        draws = jax.random.uniform(jax.random.fold_in(jax.random.fold_in(stream_key, 6), position), (parts,), jnp.float32, smallest / len(shards), high / len(shards))
        factor_of = factor_of * jnp.repeat(jnp.exp(draws), extent[position] // parts).reshape((-1,) + (1,) * (len(extent) - 1 - position))
    return factor_of


def split_up(number_of, total, most, slope):
    loads = [(1 << 20) // math.isqrt(rank ** slope) + 1 for rank in range(2, number_of + 1)]
    surplus, counts = total - most - (number_of - 1), [1] * (number_of - 1)
    while surplus > 0:
        free = [i for i in range(number_of - 1) if counts[i] < most]
        pool, budget = sum([loads[i] for i in free]), surplus
        for i in free:
            extra = min(most - counts[i], max(1, budget * loads[i] // pool), surplus)
            counts[i] = counts[i] + extra
            surplus = surplus - extra
    return np.array([most] + counts)


def ragged(stream_key, count, total, bound, slope):
    if count == 2:
        one = jax.random.randint(stream_key, (), max(1, total - bound), min(bound, total - 1) + 1)
        return jnp.stack([one, total - one])
    lengths = jnp.asarray(split_up(count, total, bound, slope), jnp.int32)
    couples = (count - 1) // 2
    source_of, receiver = lengths[1:1 + 2 * couples:2], lengths[2:2 + 2 * couples:2]
    margin = jnp.minimum(source_of - 1, bound - receiver)
    passed = jax.random.randint(jax.random.fold_in(stream_key, 1), (couples,), 0, 1 << 20) % (margin + 1)
    lengths = lengths.at[1:1 + 2 * couples:2].set(source_of - passed).at[2:2 + 2 * couples:2].set(receiver + passed)
    return lengths[jax.random.permutation(jax.random.fold_in(stream_key, 2), count)]


def centred(rng, extent, width, bound, shards=(), kind=jnp.bfloat16):
    level = block_scale(rng, extent, shards, -0.22, 0.18) if shards else 1.0
    values = jax.random.normal(rng, extent, jnp.float32) * width * level
    return jnp.minimum(jnp.maximum(values, -bound), bound).astype(kind)


def setup_inputs(seed: int = 0, part: int = 0) -> dict:
    key_of = jax.random.split(jax.random.key(seed), 15)
    own_keys = jax.random.split(jax.random.fold_in(key_of[14], part), 15)
    queries = draw_queries(jax.random.fold_in(jax.random.fold_in(key_of[14], part), 71), part)
    key_states = draw_key_states(jax.random.fold_in(jax.random.fold_in(key_of[14], part), 71), part)
    value_states = centred(own_keys[2], (CTXLEN, KVH * HD), 1.0, 6.0, ((0, 8), (1, 2)))
    out_grad = centred(own_keys[3], (CTXLEN, QH * HD), 1.0, 6.0, ((0, 8), (1, 2)))
    doc_ids = jnp.searchsorted(jnp.cumsum(ragged(own_keys[4], DOCS, NBLK, DOC_MOST, 2)), jnp.arange(NBLK), side="right").astype(jnp.int32)
    int_pos = draw_int_pos(jax.random.fold_in(jax.random.fold_in(key_of[14], part), 71), part)
    hidden = centred(own_keys[6], (POS_ALL, D), 1.0, 6.0, ((1, 8),))
    upstream = centred(own_keys[7], (POS_ALL, D), 0.2, 3.0, ((1, 8),))
    w_query = centred(key_of[8], (D, QH * HD), D ** -0.5, 0.09375, ((0, 8), (1, 2)))
    w_key = centred(key_of[9], (D, KVH * HD), D ** -0.5, 0.09375, ((0, 8), (1, 2)))
    w_value = centred(key_of[10], (D, KVH * HD), D ** -0.5, 0.09375, ((0, 8), (1, 2)))
    rotation = centred(key_of[11], (RANK, D), D ** -0.5, 0.09375, ((1, 8),), jnp.float32)
    projection = centred(key_of[12], (RANK, D), D ** -0.5, 0.09375, ((1, 8),), jnp.float32)
    rank_bias = centred(key_of[13], (RANK,), 1.0, 4.0, (), jnp.float32)
    return dict(queries=queries, key_states=key_states, value_states=value_states, out_grad=out_grad, doc_ids=doc_ids, int_pos=int_pos, hidden=hidden, upstream=upstream, w_query=w_query, w_key=w_key, w_value=w_value, rotation=rotation, projection=projection, rank_bias=rank_bias)


scale_q = 1.0 / 12.0
soft_cap = 50.0

def capping(dot_vals):
    return soft_cap * jnp.tanh(dot_vals * scale_q / soft_cap)

def reference(queries, key_states, value_states, out_grad, doc_ids, int_pos, hidden, upstream, w_query, w_key, w_value, rotation, projection, rank_bias):
    length = queries.shape[0]
    per_group = QH // KVH
    query_all = queries.reshape(length, QH, HD)
    key_all = key_states.reshape(length, KVH, HD)
    value_all = value_states.reshape(length, KVH, HD)
    grad_all = out_grad.reshape(length, QH, HD)
    tok_pos = jnp.arange(length, dtype=jnp.int32)
    tok_doc = doc_ids[tok_pos // BLK]
    pick_pos = jnp.arange(POS_ALL, dtype=jnp.int32) // POS_DEV * TOK_DEV + int_pos
    pick_doc = tok_doc[pick_pos]
    q_block = math.gcd(length, 512)
    block_count = length // q_block

    def forward_head(head_no):
        query_h = query_all[:, head_no]
        key_h = key_all[:, head_no // per_group]
        value_h = value_all[:, head_no // per_group]

        def forward_block(block_no):
            query_rows = lax.dynamic_slice_in_dim(query_h, block_no * q_block, q_block, 0)
            rows_pos = lax.dynamic_slice_in_dim(tok_pos, block_no * q_block, q_block, 0)
            rows_doc = lax.dynamic_slice_in_dim(tok_doc, block_no * q_block, q_block, 0)
            capped = capping(jnp.dot(query_rows, key_h.T, preferred_element_type=jnp.float32))
            visible = (tok_pos[None, :] <= rows_pos[:, None]) & (tok_doc[None, :] == rows_doc[:, None])
            weights = jnp.where(visible, jnp.exp(capped), 0.0)
            return (lax.optimization_barrier(jnp.sum(weights, axis=1)), jnp.dot(weights.astype(jnp.bfloat16), value_h, preferred_element_type=jnp.float32))
        z_blocks, numer_blocks = lax.map(forward_block, jnp.arange(block_count, dtype=jnp.int32))
        return (z_blocks.reshape(length), numer_blocks.reshape(length, HD))
    z_all, numer_all = lax.map(forward_head, jnp.arange(QH, dtype=jnp.int32))
    outputs = numer_all / z_all[..., None]
    row_delta = lax.optimization_barrier(jnp.sum(jnp.transpose(grad_all, (1, 0, 2)).astype(jnp.float32) * outputs, axis=-1))

    def query_grad(head_no):
        query_h = query_all[:, head_no]
        grad_h = grad_all[:, head_no]
        key_h = key_all[:, head_no // per_group]
        value_h = value_all[:, head_no // per_group]
        pick_query = query_h[pick_pos]
        pick_grad = grad_h[pick_pos]
        capped = capping(jnp.dot(pick_query, key_h.T, preferred_element_type=jnp.float32))
        visible = (tok_pos[None, :] <= pick_pos[:, None]) & (tok_doc[None, :] == pick_doc[:, None])
        weights = jnp.where(visible, jnp.exp(capped), 0.0) * (1.0 - (capped / soft_cap) ** 2)
        prob_grad = jnp.dot(pick_grad, value_h.T, preferred_element_type=jnp.float32)
        main_sum = jnp.dot((weights * prob_grad).astype(jnp.bfloat16), key_h, preferred_element_type=jnp.float32)
        side_sum = jnp.dot(weights.astype(jnp.bfloat16), key_h, preferred_element_type=jnp.float32)
        z_pick = z_all[head_no][pick_pos]
        delta_pick = row_delta[head_no][pick_pos]
        return scale_q * (main_sum - delta_pick[:, None] * side_sum) / z_pick[:, None]
    dq_heads = lax.map(query_grad, jnp.arange(QH, dtype=jnp.int32))
    dq_rows = jnp.transpose(dq_heads, (1, 0, 2)).reshape(POS_ALL, QH * HD).astype(jnp.bfloat16)

    def key_grad(head_no):
        query_h = query_all[:, head_no]
        grad_h = grad_all[:, head_no]
        key_pick = key_all[:, head_no // per_group][pick_pos]
        value_pick = value_all[:, head_no // per_group][pick_pos]
        capped = capping(jnp.dot(query_h, key_pick.T, preferred_element_type=jnp.float32))
        visible = (pick_pos[None, :] <= tok_pos[:, None]) & (pick_doc[None, :] == tok_doc[:, None])
        probs = jnp.where(visible, jnp.exp(capped), 0.0) / z_all[head_no][:, None]
        prob_grad = jnp.dot(grad_h, value_pick.T, preferred_element_type=jnp.float32)
        dscore = probs * (prob_grad - row_delta[head_no][:, None]) * (1.0 - (capped / soft_cap) ** 2)
        value_g = jnp.dot(probs.astype(jnp.bfloat16).T, grad_h, preferred_element_type=jnp.float32)
        key_g = scale_q * jnp.dot(dscore.astype(jnp.bfloat16).T, query_h, preferred_element_type=jnp.float32)
        return (key_g, value_g)
    key_heads_g, value_heads_g = lax.map(key_grad, jnp.arange(QH, dtype=jnp.int32))
    key_sum = key_heads_g.reshape(KVH, per_group, POS_ALL, HD).sum(axis=1)
    value_sum = value_heads_g.reshape(KVH, per_group, POS_ALL, HD).sum(axis=1)
    dk_rows = jnp.transpose(key_sum, (1, 0, 2)).reshape(POS_ALL, KVH * HD).astype(jnp.bfloat16)
    dv_rows = jnp.transpose(value_sum, (1, 0, 2)).reshape(POS_ALL, KVH * HD).astype(jnp.bfloat16)
    resid_grad = jnp.dot(dq_rows, w_query.T, preferred_element_type=jnp.float32)
    resid_grad = resid_grad + jnp.dot(dk_rows, w_key.T, preferred_element_type=jnp.float32)
    resid_grad = resid_grad + jnp.dot(dv_rows, w_value.T, preferred_element_type=jnp.float32)
    resid_grad = resid_grad + upstream.astype(jnp.float32)
    hidden_wide = hidden.astype(jnp.float32)
    rank_grad = jnp.dot(resid_grad, rotation.T, precision=lax.Precision.HIGHEST)
    rank_state = jnp.dot(hidden_wide, (projection - rotation).T, precision=lax.Precision.HIGHEST) + rank_bias[None, :]
    grad_bias = lax.optimization_barrier(jnp.sum(rank_grad, axis=0))
    grad_proj = jnp.dot(rank_grad.T, hidden_wide, precision=lax.Precision.HIGHEST)
    grad_rot = jnp.dot(rank_state.T, resid_grad, precision=lax.Precision.HIGHEST) - grad_proj
    return (grad_rot, grad_proj, grad_bias)
```

```python
import functools

import jax
import jax.numpy as jnp
from jax import lax
from jax.experimental import pallas as pl
from jax.experimental.pallas import tpu as pltpu
from jax.sharding import PartitionSpec as P

HD = 128
BLK = 64
POS_DEV = 8
LANES = 128

scale_q = 1.0 / 12.0
soft_cap = 50.0

MESH = pl.DeviceIdType.MESH
F32 = jnp.float32
BF16 = jnp.bfloat16


def round_up(value, multiple):
    return (value + multiple - 1) // multiple * multiple


def dot(left, right):
    return jnp.dot(left, right, preferred_element_type=F32)


def dot_nt(left, right):
    return lax.dot_general(left, right, (((1,), (1,)), ((), ())), preferred_element_type=F32)


def dot_tn(left, right):
    return lax.dot_general(left, right, (((0,), (0,)), ((), ())), preferred_element_type=F32)


def split2(x):
    hi = x.astype(BF16)
    return hi, (x - hi.astype(F32)).astype(BF16)


def split3(x):
    hi = x.astype(BF16)
    rest = x - hi.astype(F32)
    mid = rest.astype(BF16)
    low = (rest - mid.astype(F32)).astype(BF16)
    return jnp.concatenate([hi, mid, low], axis=0)


def join3(x):
    r = x.shape[0] // 3
    return x[:r] + x[r : 2 * r] + x[2 * r :]


def kernel(
    n,
    q_hbm, k_hbm, v_hbm, g_hbm, doc_hbm, pos_hbm, hidden_hbm, up_hbm,
    wq_hbm, wk_hbm, wv_hbm, rot_hbm, proj_hbm, bias_hbm,
    rot_out, proj_out, bias_out,
    kv, qb, gb, qp, gp, pp, zs, num, zp, nump, ms, kp, vp, rows_all,
    ax_out, ax_own, ax_in, az_out, az_all, t_out, t_all, sw_out, sw_in,
    wq, wk, wv, doc_ref, pos_ref, hidden_ref, up_ref, rot_ref, proj_ref, bias_ref,
    l_sem, z_send, z_recv, x_send, x_recv, xa_send, xa_recv, az_send, az_recv,
    t_send, t_recv, sw_send, sw_recv,
):
    me = lax.axis_index("ctx")
    core = lax.axis_index("head")
    pair = me // 2
    x = lax.rem(me, 2)
    partner = me + 1 - 2 * x
    npair = n // 2
    hist = npair // 2
    tokens = q_hbm.shape[0]
    span = 2 * tokens
    kw = kv.shape[3]
    qw = qb.shape[1]
    kheads = kw // HD
    npos = n * POS_DEV
    mine = 2 * POS_DEV
    lanes = round_up(npos, LANES)
    wide = qw + 2 * kw
    fold = wide // 2

    barrier = pltpu.get_barrier_semaphore()
    for k in range(1, n):
        pl.semaphore_signal(
            barrier, inc=1, device_id={"ctx": lax.rem(me + k, n)}, device_id_type=MESH
        )
    pl.semaphore_signal(barrier, inc=1, device_id={"head": 1 - core}, device_id_type=MESH)

    own_rows = pl.ds(pl.multiple_of(x * tokens, tokens), tokens)

    def cols(ref, which, width):
        return ref.at[:, pl.ds(pl.multiple_of(which * width, width), width)]

    pairs_in = (
        (cols(k_hbm, x, kw), kv.at[0, 0, own_rows]), (cols(v_hbm, x, kw), kv.at[0, 1, own_rows]),
        (doc_hbm, doc_ref), (pos_hbm, pos_ref),
        (cols(q_hbm, x, qw), qb.at[own_rows]), (cols(g_hbm, x, qw), gb.at[own_rows]),
        (rot_hbm, rot_ref), (proj_hbm, proj_ref), (hidden_hbm, hidden_ref),
        (wq_hbm, wq), (wk_hbm, wk), (wv_hbm, wv), (up_hbm, up_ref), (bias_hbm, bias_ref),
    )
    loads = [
        pltpu.make_async_copy(src, dst, l_sem.at[i]) for i, (src, dst) in enumerate(pairs_in)
    ]
    for load in loads:
        load.start()

    def send(src, dst, send_sem, recv_sem, **where):
        return pltpu.make_async_remote_copy(
            src_ref=src, dst_ref=dst, send_sem=send_sem, recv_sem=recv_sem,
            device_id=where, device_id_type=MESH,
        )

    above = lax.rem(me + 2, n)

    def z_copy(j, c, t, run, first=False):
        def go(start, size):
            rows = pl.ds(start, size)
            src = kv.at[j - 1, c, rows]
            if first:
                src = cols((k_hbm, v_hbm)[c], x, kw)
                if size < tokens:
                    src = src.at[pl.ds(tokens - size, size)]
            run(send(src, kv.at[j, c, rows], z_send.at[j - 1, c, t], z_recv.at[j - 1, c, t],
                     ctx=above))
        if j < hist:
            go(pl.multiple_of(t * tokens, tokens), tokens)
        else:
            @pl.when(t == 0)
            def _():
                go(BLK, tokens - BLK)

            @pl.when(t == 1)
            def _():
                go(tokens, tokens)

    def start(copy):
        copy.start()

    def has(j):
        return pair >= j

    def sends(j):
        return jnp.logical_and(pair >= j - 1, pair + 1 < npair)

    other = 1 - x
    x_copies = [
        send(cols(k_hbm, other, kw), kv.at[0, 0, own_rows], x_send.at[0], x_recv.at[0], ctx=partner),
        send(cols(v_hbm, other, kw), kv.at[0, 1, own_rows], x_send.at[1], x_recv.at[1], ctx=partner),
        send(cols(q_hbm, other, qw), qb.at[own_rows], x_send.at[2], x_recv.at[2], ctx=partner),
        send(cols(g_hbm, other, qw), gb.at[own_rows], x_send.at[3], x_recv.at[3], ctx=partner),
    ]

    pl.semaphore_wait(barrier, n)
    for copy in x_copies[:2]:
        copy.start()

    @pl.when(sends(1))
    def _():
        for c in range(2):
            z_copy(1, c, x, start, first=True)

    for copy in x_copies[2:]:
        copy.start()

    for load in loads[2:13]:
        load.wait()
    rot = rot_ref[...]
    rot3 = split3(rot)
    hidden = hidden_ref[...]
    up = up_ref[...]
    state = join3(dot_nt(split3(proj_ref[...] - rot), hidden))
    if lanes > npos:
        for ref in (ax_out, ax_own):
            ref[:, wide:] = jnp.zeros((ref.shape[0], lanes), F32)
    ax_out[:, wide : wide + npos] = state
    ax_own[:, wide : wide + npos] = state
    both = []
    for half in range(2):
        both.append(jnp.concatenate([
            join3(dot(rot3, wq[:, half * qw : (half + 1) * qw])),
            join3(dot(rot3, wk[:, half * kw : (half + 1) * kw])),
            join3(dot(rot3, wv[:, half * kw : (half + 1) * kw])),
        ], axis=1))
    ax_own[:, :wide] = jnp.where(x == 0, both[0], both[1])
    ax_out[:, :wide] = jnp.where(x == 0, both[1], both[0])
    xa_copy = send(ax_out, ax_in, xa_send, xa_recv, ctx=partner)
    xa_copy.start()

    for c in range(2):
        x_copies[c].wait_recv()

        @pl.when(sends(1))
        def _(c=c):
            z_copy(1, c, other, start)

    blocks = span // BLK
    docs = [doc_ref[pair * blocks + b] for b in range(blocks)]

    def count(i, carry):
        one = doc_ref[i]
        return tuple(s + jnp.where(one < d, BLK, 0) for s, d in zip(carry, docs))

    starts = lax.fori_loop(0, doc_ref.shape[0], count, (jnp.int32(0),) * blocks)
    starts = [s - pair * span for s in starts]

    def start_of(position):
        out = jnp.zeros(position.shape, jnp.int32) + starts[0]
        for b in range(1, blocks):
            out = jnp.where(position >= b * BLK, starts[b], out)
        return out

    row = lax.broadcasted_iota(jnp.int32, (span, span), 0)
    key = lax.broadcasted_iota(jnp.int32, (span, span), 1)
    row_start = start_of(row)
    lane_pos = lax.broadcasted_iota(jnp.int32, (1, npos), 1)
    pick_rel = lane_pos // POS_DEV * tokens + pos_ref[...] - pair * span
    token = lax.broadcasted_iota(jnp.int32, (span, npos), 0)

    def one_hot(j):
        return jnp.where(token - j * span == pick_rel, 1.0, 0.0).astype(BF16)

    hot = one_hot(0)
    my_picks = pl.ds(pl.multiple_of(pair * mine, mine), mine)
    pp[...] = dot_tn(hot, lax.broadcasted_iota(jnp.int32, (span, LANES), 0).astype(F32).astype(BF16))
    where_pick = pp[my_picks, :1].astype(jnp.int32)
    where_pick = jnp.concatenate([where_pick, where_pick], axis=0)
    pick_start = start_of(where_pick)

    if hist > 1:
        for c in range(2):
            @pl.when(has(1))
            def _(c=c):
                z_copy(1, c, x, lambda copy: copy.wait_recv())

            @pl.when(jnp.logical_and(has(1), sends(2)))
            def _(c=c):
                z_copy(2, c, x, start)

    for load in loads[:2]:
        load.wait()
    kv[hist, :, :BLK] = jnp.zeros((2, BLK, kw), BF16)
    kp[...] = dot_tn(hot, kv[0, 0])
    vp[...] = dot_tn(hot, kv[0, 1])

    def visit_rows(j):
        rows = span - BLK if j == hist else span
        seen = key[:rows] - j * span >= row_start[:rows]
        if j == 0:
            seen = seen & (key <= row)
        for h in range(2 * kheads):
            at = slice(h // 2 * HD, (h // 2 + 1) * HD)
            keys, values = kv[j, 0, :, at], kv[j, 1, :, at]
            bent = jnp.tanh(
                dot_nt(qb[:rows, h * HD : (h + 1) * HD], keys) * (scale_q / soft_cap)
            )
            weights = jnp.where(seen, jnp.exp(soft_cap * bent), 0.0)
            folded = weights[:, :LANES]
            for a in range(LANES, span, LANES):
                folded = folded + weights[:, a : a + LANES]
            num_new = dot(weights.astype(BF16), values)
            if j == 0:
                zs[h], num[h] = folded, num_new
            else:
                zs[h, :rows] += folded
                num[h, :rows] += num_new

    def visit_picks(j):
        key_at = key[: 2 * mine] - j * span
        seen = (key_at >= pick_start) & (key_at <= where_pick)
        if j > 0:
            hot_j = one_hot(j)
            kp[...] += dot_tn(hot_j, kv[j, 0])
            vp[...] += dot_tn(hot_j, kv[j, 1])
        for h in range(kheads):
            at = slice(h * HD, (h + 1) * HD)
            keys, values = kv[j, 0, :, at], kv[j, 1, :, at]
            bent = jnp.tanh(dot_nt(qp[h], keys) * (scale_q / soft_cap))
            weights = jnp.where(seen, jnp.exp(soft_cap * bent), 0.0)
            folded = weights[:, :LANES]
            for a in range(LANES, span, LANES):
                folded = folded + weights[:, a : a + LANES]
            num_new = dot(weights.astype(BF16), values)
            side = weights * (1.0 - bent * bent)
            main = side * dot_nt(gp[h], values)
            ms_new = dot(jnp.concatenate([main, side], axis=0).astype(BF16), keys)
            if j == 0:
                zp[h], nump[h], ms[h] = folded, num_new, ms_new
            else:
                zp[h] += folded
                nump[h] += num_new
                ms[h] += ms_new

    def arrive(j):
        for t in (x, other):
            if j == 1 and hist > 1 and t is x:
                continue
            for c in range(2):
                z_copy(j, c, t, lambda copy: copy.wait_recv())
                if j < hist:
                    @pl.when(sends(j + 1))
                    def _(c=c, t=t):
                        z_copy(j + 1, c, t, start)

    x_copies[2].wait_recv()
    visit_rows(0)

    @pl.when(has(1))
    def _():
        arrive(1)
        visit_rows(1)

    xa_copy.wait_recv()
    ax = ax_own[...] + ax_in[...]
    s_hi, s_lo = split2(ax[:, wide:])
    az_out[:, :fold] = jnp.concatenate([ax[:, :fold], ax[:, fold:wide]], axis=0).astype(BF16)
    az_out[:, fold:] = jnp.concatenate([s_hi, s_lo], axis=0)

    def az_copy(k, receive):
        slot = lax.rem(pair - k + npair, npair) if receive else pair
        return send(
            az_out, az_all.at[slot], az_send.at[k - 1], az_recv.at[slot],
            ctx=lax.rem(me + 2 * k, n),
        )

    for k in range(1, npair):
        az_copy(k, False).start()
    az_all[pair] = az_out[...]

    x_copies[3].wait_recv()
    for picked, src in ((qp, qb), (gp, gb)):
        rows_all[:, :qw] = dot_tn(hot, src[...])
        got = rows_all[my_picks, :qw].astype(BF16)
        for h in range(kheads):
            a, b, c = 2 * h * HD, (2 * h + 1) * HD, (2 * h + 2) * HD
            picked[h] = jnp.concatenate([got[:, a:b], got[:, b:c]], axis=0)
    visit_picks(0)

    @pl.when(has(1))
    def _():
        visit_picks(1)

    for j in range(2, hist + 1):
        @pl.when(has(j))
        def _(j=j):
            arrive(j)
            visit_rows(j)
            visit_picks(j)

    rows_all[:, :qw] = jnp.zeros((npos, qw), F32)
    for h in range(kheads):
        at = slice(h * HD, (h + 1) * HD)
        total = jnp.sum(zp[h], axis=1, keepdims=True)
        delta = jnp.sum(gp[h].astype(F32) * (nump[h] / total), axis=1, keepdims=True)
        main, side = ms[h, : 2 * mine], ms[h, 2 * mine :]
        dq = (scale_q * (main - delta * side) / total).astype(BF16).astype(F32)
        for i in range(2):
            rows_all[my_picks, (2 * h + i) * HD : (2 * h + i + 1) * HD] = dq[
                i * mine : (i + 1) * mine
            ]

    row1 = lax.broadcasted_iota(jnp.int32, (span, npos), 0)
    seen = (pick_rel >= start_of(row1)) & (pick_rel <= row1)
    for h in range(kheads):
        at = slice(h * HD, (h + 1) * HD)
        keys = kp[:, at].astype(BF16)
        values = vp[:, at].astype(BF16)
        dk = dv = 0.0
        for i in range(2 * h, 2 * h + 2):
            query = qb[:, i * HD : (i + 1) * HD]
            grad = gb[:, i * HD : (i + 1) * HD]
            total = jnp.sum(zs[i], axis=1, keepdims=True)
            delta = jnp.sum(grad.astype(F32) * (num[i] / total), axis=1, keepdims=True)
            bent = jnp.tanh(dot_nt(query, keys) * (scale_q / soft_cap))
            prob = jnp.where(seen, jnp.exp(soft_cap * bent), 0.0) / total
            dscore = prob * (dot_nt(grad, values) - delta) * (1.0 - bent * bent)
            dv = dv + dot_tn(prob.astype(BF16), grad)
            dk = dk + dot_tn(dscore.astype(BF16), query)
        rows_all[:, qw + h * HD : qw + (h + 1) * HD] = scale_q * dk
        rows_all[:, qw + kw + h * HD : qw + kw + (h + 1) * HD] = dv

    for k in range(1, npair):
        az_copy(k, True).wait_recv()
    az = az_all[0].astype(F32)
    for i in range(1, npair):
        az = az + az_all[i].astype(F32)
    rank = rot.shape[0]
    rank_state = az[:rank, fold : fold + npos] + az[rank:, fold : fold + npos]
    loads[13].wait()
    bias_row = lax.broadcasted_iota(jnp.int32, rank_state.shape, 0)
    for r in range(rank):
        rank_state = rank_state + jnp.where(bias_row == r, bias_ref[r], 0.0)
    rw = jnp.concatenate([az[:rank, :fold], az[rank:, :fold]], axis=1)

    r_hi, r_lo = split2(rows_all[...])
    s_hi, s_lo = split2(rank_state)
    s2 = dot(jnp.concatenate([s_hi, s_lo], axis=0), r_hi)
    term = s2[:rank] + s2[rank:] + dot(s_hi, r_lo)
    a_hi, a_lo = split2(rw)
    a2 = dot_nt(jnp.concatenate([a_hi, a_lo], axis=0), r_hi)
    rank_up = join3(dot_nt(rot3, up))
    first_core = jnp.where(core == 0, 1.0, 0.0)
    rg = a2[:rank] + a2[rank:] + dot_nt(a_hi, r_lo)

    rg = rg + first_core * rank_up
    g_hi, g_lo = split2(rg)
    if lanes > npos:
        t_out[:, fold:] = jnp.zeros((2 * rank, lanes), BF16)
    t_out[:, :fold] = jnp.concatenate([term[:, :fold], term[:, fold:]], axis=0).astype(BF16)
    t_out[:, fold : fold + npos] = jnp.concatenate([g_hi, g_lo], axis=0)

    def t_copy(k, receive):
        slot = lax.rem(me - k + n, n) if receive else me
        return send(
            t_out, t_all.at[slot], t_send.at[k - 1], t_recv.at[slot], ctx=lax.rem(me + k, n)
        )

    for k in range(1, n):
        t_copy(k, False).start()
    t_all[me] = t_out[...]
    rot_up = first_core * join3(dot(split3(rank_state), up))
    for k in range(1, n):
        t_copy(k, True).wait_recv()

    sums = []
    for i in range(2):
        total = t_all[i].astype(F32)
        for z in range(1, npair):
            total = total + t_all[2 * z + i].astype(F32)
        sums.append(total)
    rg = sums[0][:, fold : fold + npos] + sums[1][:, fold : fold + npos]
    rg = rg[:rank] + rg[rank:]
    terms = [
        jnp.concatenate([total[:rank, :fold], total[rank:, :fold]], axis=1) for total in sums
    ]

    def weighted(w, a, b):
        t = jnp.concatenate([terms[0][:, a:b], terms[1][:, a:b]], axis=1)
        return dot_nt(w[...], jnp.concatenate(split2(t), axis=0))

    res = weighted(wq, 0, qw) + weighted(wk, qw, qw + kw) + weighted(wv, qw + kw, wide)
    res = jnp.transpose(res)
    grad = res[:rank] + res[rank:] + rot_up
    grad_proj = join3(dot(split3(rg), hidden))

    width = hidden.shape[1]
    room = sw_out.shape[2]
    if room > width:
        sw_out[0] = jnp.zeros((rank, room), F32)
        sw_out[1] = jnp.zeros((rank, room), F32)
    sw_out[0, :, :width] = grad - grad_proj
    sw_out[1, :, :width] = grad_proj
    sw_out[2, :, :lanes] = jnp.broadcast_to(jnp.sum(rg, axis=1, keepdims=True), (rank, lanes))
    sw_copy = send(sw_out, sw_in, sw_send, sw_recv, head=1 - core)
    sw_copy.start()
    sw_copy.wait_recv()
    rot_out[...] = sw_out[0, :, :width] + sw_in[0, :, :width]
    proj_out[...] = sw_out[1, :, :width] + sw_in[1, :, :width]
    bias = sw_out[2, :, :lanes] + sw_in[2, :, :lanes]
    for r in range(rank):
        bias_out[r] = bias[r, 0]

    sw_copy.wait_send()
    xa_copy.wait_send()
    for copy in x_copies:
        copy.wait_send()
    for k in range(1, npair):
        az_copy(k, False).wait_send()
    for k in range(1, n):
        t_copy(k, False).wait_send()

    def sent(copy):
        copy.wait_send()

    for j in range(1, hist + 1):
        @pl.when(sends(j))
        def _(j=j):
            for c in range(2):
                z_copy(j, c, x, sent, first=j == 1)
                z_copy(j, c, other, sent)


def finish(rot_in, proj_in, bias_in, rot_out, proj_out, bias_out):
    rot_out[...] = rot_in[...]
    proj_out[...] = proj_in[...]
    bias_out[...] = bias_in[...]


def local(n, *args):
    args = list(args)
    args[5] = args[5].reshape(1, -1)
    queries, key_states = args[0], args[1]
    hidden, rotation = args[6], args[11]
    tokens, q_width = queries.shape
    kv_width = key_states.shape[1]
    qw, kw = q_width // 2, kv_width // 2
    kheads = kw // HD
    width = hidden.shape[1]
    rank = rotation.shape[0]
    npair = n // 2
    hist = npair // 2
    npos = n * POS_DEV
    mine = 2 * POS_DEV
    lanes = round_up(npos, LANES)
    span = 2 * tokens
    wide = qw + 2 * kw
    fold = wide // 2
    room = max(round_up(width, LANES), lanes)
    vmem = pl.BlockSpec(memory_space=pltpu.VMEM)
    smem = pl.BlockSpec(memory_space=pltpu.SMEM)
    hbm = pl.BlockSpec(memory_space=pltpu.HBM)
    dma = pltpu.SemaphoreType.DMA
    outs = pl.pallas_call(
        functools.partial(kernel, n),
        out_shape=(
            jax.ShapeDtypeStruct((rank, width), F32),
            jax.ShapeDtypeStruct((rank, width), F32),
            jax.ShapeDtypeStruct((rank,), F32),
        ),
        in_specs=[hbm] * len(args),
        out_specs=(vmem, vmem, smem),
        scratch_shapes=[
            pltpu.VMEM((hist + 1, 2, span, kw), BF16),
            pltpu.VMEM((span, qw), BF16),
            pltpu.VMEM((span, qw), BF16),
            pltpu.VMEM((kheads, 2 * mine, HD), BF16),
            pltpu.VMEM((kheads, 2 * mine, HD), BF16),
            pltpu.VMEM((npos, LANES), F32),
            pltpu.VMEM((2 * kheads, span, LANES), F32),
            pltpu.VMEM((2 * kheads, span, HD), F32),
            pltpu.VMEM((kheads, 2 * mine, LANES), F32),
            pltpu.VMEM((kheads, 2 * mine, HD), F32),
            pltpu.VMEM((kheads, 4 * mine, HD), F32),
            pltpu.VMEM((npos, kw), F32),
            pltpu.VMEM((npos, kw), F32),
            pltpu.VMEM((npos, wide), F32),
            pltpu.VMEM((rank, wide + lanes), F32),
            pltpu.VMEM((rank, wide + lanes), F32),
            pltpu.VMEM((rank, wide + lanes), F32),
            pltpu.VMEM((2 * rank, fold + lanes), BF16),
            pltpu.VMEM((npair, 2 * rank, fold + lanes), BF16),
            pltpu.VMEM((2 * rank, fold + lanes), BF16),
            pltpu.VMEM((n, 2 * rank, fold + lanes), BF16),
            pltpu.VMEM((3, rank, room), F32),
            pltpu.VMEM((3, rank, room), F32),
            pltpu.VMEM((width, q_width), BF16),
            pltpu.VMEM((width, kv_width), BF16),
            pltpu.VMEM((width, kv_width), BF16),
            pltpu.SMEM(args[4].shape, jnp.int32),
            pltpu.VMEM(args[5].shape, jnp.int32),
            pltpu.VMEM(hidden.shape, BF16),
            pltpu.VMEM(hidden.shape, BF16),
            pltpu.VMEM(rotation.shape, F32),
            pltpu.VMEM(rotation.shape, F32),
            pltpu.SMEM((rank,), F32),
            dma((len(args),)),
            dma((hist, 2, 2)), dma((hist, 2, 2)),
            dma((4,)), dma((4,)),
            dma, dma,
            dma((npair,)), dma((npair,)),
            dma((n,)), dma((n,)),
            dma, dma,
        ],
        compiler_params=pltpu.CompilerParams(
            collective_id=0, has_side_effects=True, vmem_limit_bytes=64 << 20
        ),
        name="rank_backward",
    )(*args)
    return pl.pallas_call(
        finish,
        out_shape=tuple(jax.ShapeDtypeStruct(out.shape, out.dtype) for out in outs),
        in_specs=[vmem] * 3,
        out_specs=(vmem,) * 3,
        name="finish",
    )(*outs)


def solution(mesh):
    in_specs = (
        P(("groups", "ctx"), "head"),
        P(("groups", "ctx"), "head"),
        P(("groups", "ctx"), "head"),
        P(("groups", "ctx"), "head"),
        P("groups"),
        P("groups"),
        P("groups", "ctx"),
        P("groups", "ctx"),
        P("ctx", "head"),
        P("ctx", "head"),
        P("ctx", "head"),
        P(None, "ctx"),
        P(None, "ctx"),
        P(),
    )
    out_specs = (P("groups", "ctx"), P("groups", "ctx"), P("groups"))
    return jax.shard_map(
        functools.partial(local, mesh.shape["ctx"]),
        mesh=mesh, in_specs=in_specs, out_specs=out_specs, check_vma=False,
    )
```

```python
import functools

import jax
import jax.numpy as jnp
from jax import lax
from jax.experimental import pallas as pl
from jax.experimental.pallas import tpu as pltpu
from jax.sharding import PartitionSpec as P

HD = 128
BLK = 64
POS_DEV = 8
LANES = 128

scale_q = 1.0 / 12.0
soft_cap = 50.0

MESH = pl.DeviceIdType.MESH
F32 = jnp.float32
BF16 = jnp.bfloat16


def round_up(value, multiple):
    return (value + multiple - 1) // multiple * multiple


def dot(left, right):
    return jnp.dot(left, right, preferred_element_type=F32)


def dot_nt(left, right):
    return lax.dot_general(left, right, (((1,), (1,)), ((), ())), preferred_element_type=F32)


def dot_tn(left, right):
    return lax.dot_general(left, right, (((0,), (0,)), ((), ())), preferred_element_type=F32)


def split2(x):
    hi = x.astype(BF16)
    return hi, (x - hi.astype(F32)).astype(BF16)


def split3(x):
    hi = x.astype(BF16)
    rest = x - hi.astype(F32)
    mid = rest.astype(BF16)
    low = (rest - mid.astype(F32)).astype(BF16)
    return jnp.concatenate([hi, mid, low], axis=0)


def join3(x):
    r = x.shape[0] // 3
    return x[:r] + x[r : 2 * r] + x[2 * r :]


def kernel(
    n,
    q_hbm, k_hbm, v_hbm, g_hbm, doc_hbm, pos_hbm, hidden_hbm, up_hbm,
    wq_hbm, wk_hbm, wv_hbm, rot_hbm, proj_hbm, bias_hbm,
    rot_out, proj_out, bias_out,
    kv, qb, gb, qp, gp, pp, zs, num, zp, nump, ms, sides, kp, vp, rows_all,
    ax_out, ax_own, ax_in, az_out, az_all, tq_out, tq_all, t_out, t_all, sw_out, sw_in,
    st_out, st_in, sz_out, sz_all, rg_out, rg_all,
    wq, wk, wv, doc_ref, pos_ref, hidden_ref, up_ref, rot_ref, proj_ref, bias_ref,
    l_sem, z_send, z_recv, x_send, x_recv, xa_send, xa_recv, az_send, az_recv,
    tq_send, tq_recv, t_send, t_recv, sw_send, sw_recv,
    st_send, st_recv, sz_send, sz_recv, rg_send, rg_recv,
):
    me = lax.axis_index("ctx")
    core = lax.axis_index("head")
    pair = me // 2
    x = lax.rem(me, 2)
    partner = me + 1 - 2 * x
    npair = n // 2
    hist = npair // 2
    tokens = q_hbm.shape[0]
    span = 2 * tokens
    kw = kv.shape[3]
    qw = qb.shape[1]
    kheads = kw // HD
    npos = n * POS_DEV
    mine = 2 * POS_DEV
    lanes = round_up(npos, LANES)
    wide = qw + 2 * kw
    fold = wide // 2

    barrier = pltpu.get_barrier_semaphore()
    for k in range(1, n):
        pl.semaphore_signal(
            barrier, inc=1, device_id={"ctx": lax.rem(me + k, n)}, device_id_type=MESH
        )
    pl.semaphore_signal(barrier, inc=1, device_id={"head": 1 - core}, device_id_type=MESH)

    own_rows = pl.ds(pl.multiple_of(x * tokens, tokens), tokens)

    def cols(ref, which, width):
        return ref.at[:, pl.ds(pl.multiple_of(which * width, width), width)]

    pairs_in = (
        (cols(k_hbm, x, kw), kv.at[0, 0, own_rows]), (cols(v_hbm, x, kw), kv.at[0, 1, own_rows]),
        (doc_hbm, doc_ref), (pos_hbm, pos_ref),
        (cols(q_hbm, x, qw), qb.at[own_rows]), (cols(g_hbm, x, qw), gb.at[own_rows]),
        (rot_hbm, rot_ref), (proj_hbm, proj_ref), (hidden_hbm, hidden_ref),
        (wq_hbm, wq), (wk_hbm, wk), (wv_hbm, wv), (up_hbm, up_ref), (bias_hbm, bias_ref),
    )
    loads = [
        pltpu.make_async_copy(src, dst, l_sem.at[i]) for i, (src, dst) in enumerate(pairs_in)
    ]
    for load in loads:
        load.start()

    def send(src, dst, send_sem, recv_sem, **where):
        return pltpu.make_async_remote_copy(
            src_ref=src, dst_ref=dst, send_sem=send_sem, recv_sem=recv_sem,
            device_id=where, device_id_type=MESH,
        )

    above = lax.rem(me + 2, n)

    def z_copy(j, c, t, run, first=False):
        def go(start, size):
            rows = pl.ds(start, size)
            src = kv.at[j - 1, c, rows]
            if first:
                src = cols((k_hbm, v_hbm)[c], x, kw)
                if size < tokens:
                    src = src.at[pl.ds(tokens - size, size)]
            run(send(src, kv.at[j, c, rows], z_send.at[j - 1, c, t], z_recv.at[j - 1, c, t],
                     ctx=above))
        if j < hist:
            go(pl.multiple_of(t * tokens, tokens), tokens)
        else:
            @pl.when(t == 0)
            def _():
                go(BLK, tokens - BLK)

            @pl.when(t == 1)
            def _():
                go(tokens, tokens)

    def start(copy):
        copy.start()

    def has(j):
        return pair >= j

    def sends(j):
        return jnp.logical_and(pair >= j - 1, pair + 1 < npair)

    other = 1 - x
    x_copies = [
        send(cols(k_hbm, other, kw), kv.at[0, 0, own_rows], x_send.at[0], x_recv.at[0], ctx=partner),
        send(cols(v_hbm, other, kw), kv.at[0, 1, own_rows], x_send.at[1], x_recv.at[1], ctx=partner),
        send(cols(q_hbm, other, qw), qb.at[own_rows], x_send.at[2], x_recv.at[2], ctx=partner),
        send(cols(g_hbm, other, qw), gb.at[own_rows], x_send.at[3], x_recv.at[3], ctx=partner),
    ]

    pl.semaphore_wait(barrier, n)
    for copy in x_copies[:2]:
        copy.start()

    @pl.when(sends(1))
    def _():
        for c in range(2):
            z_copy(1, c, x, start, first=True)

    for load in loads[2:9]:
        load.wait()
    rot = rot_ref[...]
    rank = rot.shape[0]
    rot3 = split3(rot)
    hidden = hidden_ref[...]
    if lanes > npos:
        st_out[...] = jnp.zeros(st_out.shape, F32)
    st_out[:, :npos] = join3(dot_nt(split3(proj_ref[...] - rot), hidden))
    st_copy = send(st_out, st_in, st_send, st_recv, ctx=partner)
    st_copy.start()
    x_copies[2].start()
    for load in loads[9:13]:
        load.wait()
    up = up_ref[...]
    both = []
    for half in range(2):
        both.append(jnp.concatenate([
            join3(dot(rot3, wq[:, half * qw : (half + 1) * qw])),
            join3(dot(rot3, wk[:, half * kw : (half + 1) * kw])),
            join3(dot(rot3, wv[:, half * kw : (half + 1) * kw])),
        ], axis=1))

    def packed(product):
        return jnp.concatenate([product[:, :fold], product[:, fold:]], axis=0)

    ax_out[...] = packed(jnp.where(x == 0, both[1], both[0])).astype(BF16)
    xa_copy = send(ax_out, ax_in, xa_send, xa_recv, ctx=partner)
    xa_copy.start()
    x_copies[3].start()
    ax_own[...] = packed(jnp.where(x == 0, both[0], both[1]))

    for c in range(2):
        x_copies[c].wait_recv()

        @pl.when(sends(1))
        def _(c=c):
            z_copy(1, c, other, start)

    def to_pairs(src, dst, send_sem, recv_sem):
        def copy(k, receive):
            slot = lax.rem(pair - k + npair, npair) if receive else pair
            return send(
                src, dst.at[slot], send_sem.at[k - 1], recv_sem.at[slot],
                ctx=lax.rem(me + 2 * k, n),
            )
        return copy

    st_copy.wait_recv()
    sz_out[...] = jnp.concatenate(split2(st_out[...] + st_in[...]), axis=0)
    sz_copy = to_pairs(sz_out, sz_all, sz_send, sz_recv)
    for k in range(1, npair):
        sz_copy(k, False).start()
    sz_all[pair] = sz_out[...]

    blocks = span // BLK
    docs = [doc_ref[pair * blocks + b] for b in range(blocks)]

    def count(i, carry):
        one = doc_ref[i]
        return tuple(s + jnp.where(one < d, BLK, 0) for s, d in zip(carry, docs))

    starts = lax.fori_loop(0, doc_ref.shape[0], count, (jnp.int32(0),) * blocks)
    starts = [s - pair * span for s in starts]

    def start_of(position):
        out = jnp.zeros(position.shape, jnp.int32) + starts[0]
        for b in range(1, blocks):
            out = jnp.where(position >= b * BLK, starts[b], out)
        return out

    row = lax.broadcasted_iota(jnp.int32, (span, span), 0)
    key = lax.broadcasted_iota(jnp.int32, (span, span), 1)
    row_start = start_of(row)
    lane_pos = lax.broadcasted_iota(jnp.int32, (1, npos), 1)
    pick_rel = lane_pos // POS_DEV * tokens + pos_ref[...] - pair * span
    token = lax.broadcasted_iota(jnp.int32, (span, npos), 0)

    def one_hot(j):
        return jnp.where(token - j * span == pick_rel, 1.0, 0.0).astype(BF16)

    hot = one_hot(0)
    my_picks = pl.ds(pl.multiple_of(pair * mine, mine), mine)
    pp[...] = dot_tn(hot, lax.broadcasted_iota(jnp.int32, (span, LANES), 0).astype(F32).astype(BF16))
    where_pick = pp[my_picks, :1].astype(jnp.int32)
    where_pick = jnp.concatenate([where_pick, where_pick], axis=0)
    pick_start = start_of(where_pick)

    if hist > 1:
        for c in range(2):
            @pl.when(has(1))
            def _(c=c):
                z_copy(1, c, x, lambda copy: copy.wait_recv())

            @pl.when(jnp.logical_and(has(1), sends(2)))
            def _(c=c):
                z_copy(2, c, x, start)

    for load in loads[:2]:
        load.wait()
    kv[hist, :, :BLK] = jnp.zeros((2, BLK, kw), BF16)
    kp[...] = dot_tn(hot, kv[0, 0])
    vp[...] = dot_tn(hot, kv[0, 1])

    def visit_rows(j):
        rows = span - BLK if j == hist else span
        seen = key[:rows] - j * span >= row_start[:rows]
        if j == 0:
            seen = seen & (key <= row)
        for h in range(2 * kheads):
            at = slice(h // 2 * HD, (h // 2 + 1) * HD)
            keys, values = kv[j, 0, :, at], kv[j, 1, :, at]
            bent = jnp.tanh(
                dot_nt(qb[:rows, h * HD : (h + 1) * HD], keys) * (scale_q / soft_cap)
            )
            weights = jnp.where(seen, jnp.exp(soft_cap * bent), 0.0)
            folded = weights[:, :LANES]
            for a in range(LANES, span, LANES):
                folded = folded + weights[:, a : a + LANES]
            num_new = dot(weights.astype(BF16), values)
            if j == 0:
                zs[h], num[h] = folded, num_new
            else:
                zs[h, :rows] += folded
                num[h, :rows] += num_new

    def visit_picks(j):
        key_at = key[: 2 * mine] - j * span
        seen = (key_at >= pick_start) & (key_at <= where_pick)
        if j > 0:
            hot_j = one_hot(j)
            kp[...] += dot_tn(hot_j, kv[j, 0])
            vp[...] += dot_tn(hot_j, kv[j, 1])
        for h in range(kheads):
            at = slice(h * HD, (h + 1) * HD)
            keys, values = kv[j, 0, :, at], kv[j, 1, :, at]
            bent = jnp.tanh(dot_nt(qp[h], keys) * (scale_q / soft_cap))
            weights = jnp.where(seen, jnp.exp(soft_cap * bent), 0.0)
            folded = weights[:, :LANES]
            for a in range(LANES, span, LANES):
                folded = folded + weights[:, a : a + LANES]
            num_new = dot(weights.astype(BF16), values)
            side = weights * (1.0 - bent * bent)
            sides[h, j] = side
            ms_new = dot(side.astype(BF16), keys)
            if j == 0:
                zp[h], nump[h], ms[h, 2 * mine :] = folded, num_new, ms_new
            else:
                zp[h] += folded
                nump[h] += num_new
                ms[h, 2 * mine :] += ms_new

    def visit_main(j):
        for h in range(kheads):
            at = slice(h * HD, (h + 1) * HD)
            main = (sides[h, j] * dot_nt(gp[h], kv[j, 1, :, at])).astype(BF16)
            ms_new = dot(main, kv[j, 0, :, at])
            if j == 0:
                ms[h, : 2 * mine] = ms_new
            else:
                ms[h, : 2 * mine] += ms_new

    def arrive(j):
        for t in (x, other):
            if j == 1 and hist > 1 and t is x:
                continue
            for c in range(2):
                z_copy(j, c, t, lambda copy: copy.wait_recv())
                if j < hist:
                    @pl.when(sends(j + 1))
                    def _(c=c, t=t):
                        z_copy(j + 1, c, t, start)

    @pl.when(has(1))
    def _():
        arrive(1)

    def pick_rows(picked, src):
        rows_all[:, :qw] = dot_tn(hot, src[...])
        got = rows_all[my_picks, :qw].astype(BF16)
        for h in range(kheads):
            a, b, c = 2 * h * HD, (2 * h + 1) * HD, (2 * h + 2) * HD
            picked[h] = jnp.concatenate([got[:, a:b], got[:, b:c]], axis=0)

    x_copies[2].wait_recv()
    pick_rows(qp, qb)
    visit_rows(0)

    @pl.when(has(1))
    def _():
        visit_rows(1)

    xa_copy.wait_recv()
    az_out[...] = (ax_own[...] + ax_in[...].astype(F32)).astype(BF16)
    az_copy = to_pairs(az_out, az_all, az_send, az_recv)
    for k in range(1, npair):
        az_copy(k, False).start()
    az_all[pair] = az_out[...]

    visit_picks(0)

    @pl.when(has(1))
    def _():
        visit_picks(1)

    x_copies[3].wait_recv()
    pick_rows(gp, gb)
    visit_main(0)

    @pl.when(has(1))
    def _():
        visit_main(1)

    for j in range(2, hist + 1):
        @pl.when(has(j))
        def _(j=j):
            arrive(j)
            visit_rows(j)
            visit_picks(j)
            visit_main(j)

    rows_all[:, :qw] = jnp.zeros((npos, qw), F32)
    for h in range(kheads):
        at = slice(h * HD, (h + 1) * HD)
        total = jnp.sum(zp[h], axis=1, keepdims=True)
        delta = jnp.sum(gp[h].astype(F32) * (nump[h] / total), axis=1, keepdims=True)
        main, side = ms[h, : 2 * mine], ms[h, 2 * mine :]
        dq = (scale_q * (main - delta * side) / total).astype(BF16).astype(F32)
        for i in range(2):
            rows_all[my_picks, (2 * h + i) * HD : (2 * h + i + 1) * HD] = dq[
                i * mine : (i + 1) * mine
            ]

    for k in range(1, npair):
        sz_copy(k, True).wait_recv()
    sz = sz_all[0].astype(F32)
    for i in range(1, npair):
        sz = sz + sz_all[i].astype(F32)
    rank_state = sz[:rank, :npos] + sz[rank:, :npos]
    loads[13].wait()
    bias_row = lax.broadcasted_iota(jnp.int32, rank_state.shape, 0)
    for r in range(rank):
        rank_state = rank_state + jnp.where(bias_row == r, bias_ref[r], 0.0)

    s_hi, s_lo = split2(rank_state)
    s_both = jnp.concatenate([s_hi, s_lo], axis=0)
    q_rows = rows_all[:, :qw].astype(BF16)
    q2 = dot(s_both, q_rows)
    term = q2[:rank] + q2[rank:]
    tq_out[...] = jnp.concatenate([term[:, : qw // 2], term[:, qw // 2 :]], axis=0).astype(BF16)

    def to_all(src, dst, send_sem, recv_sem):
        def each(run):
            for d in range(n):
                @pl.when(me != d)
                def _(d=d):
                    run(d)

        def begin():
            each(lambda d: send(
                src, dst.at[me], send_sem.at[d], recv_sem.at[me], ctx=d
            ).start())

        def received():
            each(lambda d: send(
                src, dst.at[d], send_sem.at[d], recv_sem.at[d], ctx=d
            ).wait_recv())

        def gone():
            each(lambda d: send(
                src, dst.at[me], send_sem.at[d], recv_sem.at[me], ctx=d
            ).wait_send())

        return begin, received, gone

    tq_begin, tq_received, tq_gone = to_all(tq_out, tq_all, tq_send, tq_recv)
    tq_begin()
    tq_all[me] = tq_out[...]

    row1 = lax.broadcasted_iota(jnp.int32, (span, npos), 0)
    seen = (pick_rel >= start_of(row1)) & (pick_rel <= row1)
    for h in range(kheads):
        at = slice(h * HD, (h + 1) * HD)
        keys = kp[:, at].astype(BF16)
        values = vp[:, at].astype(BF16)
        dk = dv = 0.0
        for i in range(2 * h, 2 * h + 2):
            query = qb[:, i * HD : (i + 1) * HD]
            grad = gb[:, i * HD : (i + 1) * HD]
            total = jnp.sum(zs[i], axis=1, keepdims=True)
            delta = jnp.sum(grad.astype(F32) * (num[i] / total), axis=1, keepdims=True)
            bent = jnp.tanh(dot_nt(query, keys) * (scale_q / soft_cap))
            prob = jnp.where(seen, jnp.exp(soft_cap * bent), 0.0) / total
            dscore = prob * (dot_nt(grad, values) - delta) * (1.0 - bent * bent)
            dv = dv + dot_tn(prob.astype(BF16), grad)
            dk = dk + dot_tn(dscore.astype(BF16), query)
        rows_all[:, qw + h * HD : qw + (h + 1) * HD] = scale_q * dk
        rows_all[:, qw + kw + h * HD : qw + kw + (h + 1) * HD] = dv

    r_hi, r_lo = split2(rows_all[:, qw:])
    k2 = dot(s_both, r_hi)
    term = k2[:rank] + k2[rank:] + dot(s_hi, r_lo)
    t_out[...] = jnp.concatenate([term[:, :kw], term[:, kw:]], axis=0).astype(BF16)
    t_begin, t_received, t_gone = to_all(t_out, t_all, t_send, t_recv)
    t_begin()
    t_all[me] = t_out[...]

    rank_up = join3(dot_nt(rot3, up))
    first_core = jnp.where(core == 0, 1.0, 0.0)
    for k in range(1, npair):
        az_copy(k, True).wait_recv()
    az = az_all[0].astype(F32)
    for i in range(1, npair):
        az = az + az_all[i].astype(F32)
    rw = jnp.concatenate([az[:rank], az[rank:]], axis=1)
    a_hi, a_lo = split2(rw)
    a_both = jnp.concatenate([a_hi, a_lo], axis=0)
    a2 = dot_nt(a_both[:, :qw], q_rows) + dot_nt(a_both[:, qw:], r_hi)
    rg = a2[:rank] + a2[rank:] + dot_nt(a_hi[:, qw:], r_lo) + first_core * rank_up
    if lanes > npos:
        rg_out[...] = jnp.zeros(rg_out.shape, F32)
    rg_out[:, :npos] = rg
    rg_begin, rg_received, rg_gone = to_all(rg_out, rg_all, rg_send, rg_recv)
    rg_begin()
    rg_all[me] = rg_out[...]
    rot_up = first_core * join3(dot(split3(rank_state), up))

    def sum_over_pairs(ref):
        sums = []
        for i in range(2):
            total = ref[i].astype(F32)
            for z in range(1, npair):
                total = total + ref[2 * z + i].astype(F32)
            sums.append(total)
        return sums

    def weighted(w, parts):
        return dot_nt(w[...], jnp.concatenate(split2(jnp.concatenate(parts, axis=1)), axis=0))

    tq_received()
    res = weighted(
        wq, [p for s in sum_over_pairs(tq_all) for p in (s[:rank], s[rank:])]
    )
    t_received()
    sums = sum_over_pairs(t_all)
    res = res + weighted(wk, [s[:rank, :kw] for s in sums])
    res = res + weighted(wv, [s[rank:, :kw] for s in sums])
    res = jnp.transpose(res)
    grad = res[:rank] + res[rank:] + rot_up
    rg_received()
    rg = rg_all[0]
    for i in range(1, n):
        rg = rg + rg_all[i]
    rg = rg[:, :npos]
    grad_proj = join3(dot(split3(rg), hidden))

    width = hidden.shape[1]
    room = sw_out.shape[2]
    if room > width:
        sw_out[0] = jnp.zeros((rank, room), F32)
        sw_out[1] = jnp.zeros((rank, room), F32)
    sw_out[0, :, :width] = grad - grad_proj
    sw_out[1, :, :width] = grad_proj
    sw_out[2, :, :lanes] = jnp.broadcast_to(jnp.sum(rg, axis=1, keepdims=True), (rank, lanes))
    sw_copy = send(sw_out, sw_in, sw_send, sw_recv, head=1 - core)
    sw_copy.start()
    sw_copy.wait_recv()
    rot_out[...] = sw_out[0, :, :width] + sw_in[0, :, :width]
    proj_out[...] = sw_out[1, :, :width] + sw_in[1, :, :width]
    bias = sw_out[2, :, :lanes] + sw_in[2, :, :lanes]
    for r in range(rank):
        bias_out[r] = bias[r, 0]

    sw_copy.wait_send()
    xa_copy.wait_send()
    for copy in x_copies:
        copy.wait_send()
    for k in range(1, npair):
        az_copy(k, False).wait_send()
        sz_copy(k, False).wait_send()
    st_copy.wait_send()
    rg_gone()
    tq_gone()
    t_gone()

    def sent(copy):
        copy.wait_send()

    for j in range(1, hist + 1):
        @pl.when(sends(j))
        def _(j=j):
            for c in range(2):
                z_copy(j, c, x, sent, first=j == 1)
                z_copy(j, c, other, sent)


def finish(rot_in, proj_in, bias_in, rot_out, proj_out, bias_out):
    rot_out[...] = rot_in[...]
    proj_out[...] = proj_in[...]
    bias_out[...] = bias_in[...]


def local(n, *args):
    args = list(args)
    args[5] = args[5].reshape(1, -1)
    queries, key_states = args[0], args[1]
    hidden, rotation = args[6], args[11]
    tokens, q_width = queries.shape
    kv_width = key_states.shape[1]
    qw, kw = q_width // 2, kv_width // 2
    kheads = kw // HD
    width = hidden.shape[1]
    rank = rotation.shape[0]
    npair = n // 2
    hist = npair // 2
    npos = n * POS_DEV
    mine = 2 * POS_DEV
    lanes = round_up(npos, LANES)
    span = 2 * tokens
    wide = qw + 2 * kw
    fold = wide // 2
    room = max(round_up(width, LANES), lanes)
    vmem = pl.BlockSpec(memory_space=pltpu.VMEM)
    smem = pl.BlockSpec(memory_space=pltpu.SMEM)
    hbm = pl.BlockSpec(memory_space=pltpu.HBM)
    dma = pltpu.SemaphoreType.DMA
    outs = pl.pallas_call(
        functools.partial(kernel, n),
        out_shape=(
            jax.ShapeDtypeStruct((rank, width), F32),
            jax.ShapeDtypeStruct((rank, width), F32),
            jax.ShapeDtypeStruct((rank,), F32),
        ),
        in_specs=[hbm] * len(args),
        out_specs=(vmem, vmem, smem),
        scratch_shapes=[
            pltpu.VMEM((hist + 1, 2, span, kw), BF16),
            pltpu.VMEM((span, qw), BF16),
            pltpu.VMEM((span, qw), BF16),
            pltpu.VMEM((kheads, 2 * mine, HD), BF16),
            pltpu.VMEM((kheads, 2 * mine, HD), BF16),
            pltpu.VMEM((npos, LANES), F32),
            pltpu.VMEM((2 * kheads, span, LANES), F32),
            pltpu.VMEM((2 * kheads, span, HD), F32),
            pltpu.VMEM((kheads, 2 * mine, LANES), F32),
            pltpu.VMEM((kheads, 2 * mine, HD), F32),
            pltpu.VMEM((kheads, 4 * mine, HD), F32),
            pltpu.VMEM((kheads, hist + 1, 2 * mine, span), F32),
            pltpu.VMEM((npos, kw), F32),
            pltpu.VMEM((npos, kw), F32),
            pltpu.VMEM((npos, wide), F32),
            pltpu.VMEM((2 * rank, fold), BF16),
            pltpu.VMEM((2 * rank, fold), F32),
            pltpu.VMEM((2 * rank, fold), BF16),
            pltpu.VMEM((2 * rank, fold), BF16),
            pltpu.VMEM((npair, 2 * rank, fold), BF16),
            pltpu.VMEM((2 * rank, qw // 2), BF16),
            pltpu.VMEM((n, 2 * rank, qw // 2), BF16),
            pltpu.VMEM((2 * rank, kw), BF16),
            pltpu.VMEM((n, 2 * rank, kw), BF16),
            pltpu.VMEM((3, rank, room), F32),
            pltpu.VMEM((3, rank, room), F32),
            pltpu.VMEM((rank, lanes), F32),
            pltpu.VMEM((rank, lanes), F32),
            pltpu.VMEM((2 * rank, lanes), BF16),
            pltpu.VMEM((npair, 2 * rank, lanes), BF16),
            pltpu.VMEM((rank, lanes), F32),
            pltpu.VMEM((n, rank, lanes), F32),
            pltpu.VMEM((width, q_width), BF16),
            pltpu.VMEM((width, kv_width), BF16),
            pltpu.VMEM((width, kv_width), BF16),
            pltpu.SMEM(args[4].shape, jnp.int32),
            pltpu.VMEM(args[5].shape, jnp.int32),
            pltpu.VMEM(hidden.shape, BF16),
            pltpu.VMEM(hidden.shape, BF16),
            pltpu.VMEM(rotation.shape, F32),
            pltpu.VMEM(rotation.shape, F32),
            pltpu.SMEM((rank,), F32),
            dma((len(args),)),
            dma((hist, 2, 2)), dma((hist, 2, 2)),
            dma((4,)), dma((4,)),
            dma, dma,
            dma((npair,)), dma((npair,)),
            dma((n,)), dma((n,)),
            dma((n,)), dma((n,)),
            dma, dma,
            dma, dma,
            dma((npair,)), dma((npair,)),
            dma((n,)), dma((n,)),
        ],
        compiler_params=pltpu.CompilerParams(
            collective_id=0, has_side_effects=True, vmem_limit_bytes=64 << 20
        ),
        name="rank_backward",
    )(*args)
    return pl.pallas_call(
        finish,
        out_shape=tuple(jax.ShapeDtypeStruct(out.shape, out.dtype) for out in outs),
        in_specs=[vmem] * 3,
        out_specs=(vmem,) * 3,
        name="finish",
    )(*outs)


def solution(mesh):
    in_specs = (
        P(("groups", "ctx"), "head"),
        P(("groups", "ctx"), "head"),
        P(("groups", "ctx"), "head"),
        P(("groups", "ctx"), "head"),
        P("groups"),
        P("groups"),
        P("groups", "ctx"),
        P("groups", "ctx"),
        P("ctx", "head"),
        P("ctx", "head"),
        P("ctx", "head"),
        P(None, "ctx"),
        P(None, "ctx"),
        P(),
    )
    out_specs = (P("groups", "ctx"), P("groups", "ctx"), P("groups"))
    return jax.shard_map(
        functools.partial(local, mesh.shape["ctx"]),
        mesh=mesh, in_specs=in_specs, out_specs=out_specs, check_vma=False,
    )
```

```python
import functools

import jax
import jax.numpy as jnp
from jax import lax
from jax.experimental import pallas as pl
from jax.experimental.pallas import tpu as pltpu
from jax.sharding import PartitionSpec as P

HD = 128
BLK = 64
POS_DEV = 8
LANES = 128

scale_q = 1.0 / 12.0
soft_cap = 50.0

MESH = pl.DeviceIdType.MESH
F32 = jnp.float32
BF16 = jnp.bfloat16


def round_up(value, multiple):
    return (value + multiple - 1) // multiple * multiple


def dot(left, right):
    return jnp.dot(left, right, preferred_element_type=F32)


def dot_nt(left, right):
    return lax.dot_general(left, right, (((1,), (1,)), ((), ())), preferred_element_type=F32)


def dot_tn(left, right):
    return lax.dot_general(left, right, (((0,), (0,)), ((), ())), preferred_element_type=F32)


def split2(x):
    hi = x.astype(BF16)
    return hi, (x - hi.astype(F32)).astype(BF16)


def split3(x):
    hi = x.astype(BF16)
    rest = x - hi.astype(F32)
    mid = rest.astype(BF16)
    low = (rest - mid.astype(F32)).astype(BF16)
    return jnp.concatenate([hi, mid, low], axis=0)


def join3(x):
    r = x.shape[0] // 3
    return x[:r] + x[r : 2 * r] + x[2 * r :]


def kernel(
    n,
    q_hbm, k_hbm, v_hbm, g_hbm, doc_hbm, pos_hbm, hidden_hbm, up_hbm,
    wq_hbm, wk_hbm, wv_hbm, rot_hbm, proj_hbm, bias_hbm,
    rot_out, proj_out, bias_out,
    kv, qb, gb, qp, gp, pp, zs, num, zp, nump, ms, sides, kp, vp, rows_all,
    ax_out, ax_own, ax_in, az_out, az_all, tq_out, tq_all, t_out, t_all, sw_out, sw_in,
    st_out, st_in, sz_out, sz_all, rg_out, rg_all,
    wq, wk, wv, doc_ref, pos_ref, hidden_ref, up_ref, rot_ref, proj_ref, bias_ref,
    l_sem, z_send, z_recv, x_send, x_recv, xa_send, xa_recv, az_send, az_recv,
    tq_send, tq_recv, t_send, t_recv, sw_send, sw_recv,
    st_send, st_recv, sz_send, sz_recv, rg_send, rg_recv,
):
    me = lax.axis_index("ctx")
    core = lax.axis_index("head")
    pair = me // 2
    x = lax.rem(me, 2)
    partner = me + 1 - 2 * x
    npair = n // 2
    hist = npair // 2
    tokens = q_hbm.shape[0]
    span = 2 * tokens
    kw = kv.shape[3]
    qw = qb.shape[1]
    kheads = kw // HD
    npos = n * POS_DEV
    mine = 2 * POS_DEV
    lanes = round_up(npos, LANES)
    wide = qw + 2 * kw
    fold = wide // 2

    barrier = pltpu.get_barrier_semaphore()
    for k in range(1, n):
        pl.semaphore_signal(
            barrier, inc=1, device_id={"ctx": lax.rem(me + k, n)}, device_id_type=MESH
        )
    pl.semaphore_signal(barrier, inc=1, device_id={"head": 1 - core}, device_id_type=MESH)

    own_rows = pl.ds(pl.multiple_of(x * tokens, tokens), tokens)

    def cols(ref, which, width):
        return ref.at[:, pl.ds(pl.multiple_of(which * width, width), width)]

    pairs_in = (
        (cols(k_hbm, x, kw), kv.at[0, 0, own_rows]), (cols(v_hbm, x, kw), kv.at[0, 1, own_rows]),
        (doc_hbm, doc_ref), (pos_hbm, pos_ref),
        (cols(q_hbm, x, qw), qb.at[own_rows]), (cols(g_hbm, x, qw), gb.at[own_rows]),
        (rot_hbm, rot_ref), (proj_hbm, proj_ref), (hidden_hbm, hidden_ref),
        (wq_hbm, wq), (wk_hbm, wk), (wv_hbm, wv), (up_hbm, up_ref), (bias_hbm, bias_ref),
    )
    loads = [
        pltpu.make_async_copy(src, dst, l_sem.at[i]) for i, (src, dst) in enumerate(pairs_in)
    ]
    for load in loads:
        load.start()

    def send(src, dst, send_sem, recv_sem, **where):
        return pltpu.make_async_remote_copy(
            src_ref=src, dst_ref=dst, send_sem=send_sem, recv_sem=recv_sem,
            device_id=where, device_id_type=MESH,
        )

    above = lax.rem(me + 2, n)

    def z_copy(j, c, t, run, first=False):
        def go(start, size):
            rows = pl.ds(start, size)
            src = kv.at[j - 1, c, rows]
            if first:
                src = cols((k_hbm, v_hbm)[c], x, kw)
                if size < tokens:
                    src = src.at[pl.ds(tokens - size, size)]
            run(send(src, kv.at[j, c, rows], z_send.at[j - 1, c, t], z_recv.at[j - 1, c, t],
                     ctx=above))
        if j < hist:
            go(pl.multiple_of(t * tokens, tokens), tokens)
        else:
            @pl.when(t == 0)
            def _():
                go(BLK, tokens - BLK)

            @pl.when(t == 1)
            def _():
                go(tokens, tokens)

    def start(copy):
        copy.start()

    def has(j):
        return pair >= j

    def sends(j):
        return jnp.logical_and(pair >= j - 1, pair + 1 < npair)

    other = 1 - x
    x_copies = [
        send(cols(k_hbm, other, kw), kv.at[0, 0, own_rows], x_send.at[0], x_recv.at[0], ctx=partner),
        send(cols(v_hbm, other, kw), kv.at[0, 1, own_rows], x_send.at[1], x_recv.at[1], ctx=partner),
        send(cols(q_hbm, other, qw), qb.at[own_rows], x_send.at[2], x_recv.at[2], ctx=partner),
        send(cols(g_hbm, other, qw), gb.at[own_rows], x_send.at[3], x_recv.at[3], ctx=partner),
    ]

    pl.semaphore_wait(barrier, n)
    for copy in x_copies[:2]:
        copy.start()

    @pl.when(sends(1))
    def _():
        for c in range(2):
            z_copy(1, c, x, start, first=True)

    for load in loads[2:9]:
        load.wait()
    rot = rot_ref[...]
    rank = rot.shape[0]
    rot3 = split3(rot)
    hidden = hidden_ref[...]
    if lanes > npos:
        st_out[...] = jnp.zeros(st_out.shape, F32)
    st_out[:, :npos] = join3(dot_nt(split3(proj_ref[...] - rot), hidden))
    st_copy = send(st_out, st_in, st_send, st_recv, ctx=partner)
    st_copy.start()
    x_copies[2].start()
    for load in loads[9:13]:
        load.wait()
    up = up_ref[...]
    both = []
    for half in range(2):
        both.append(jnp.concatenate([
            join3(dot(rot3, wq[:, half * qw : (half + 1) * qw])),
            join3(dot(rot3, wk[:, half * kw : (half + 1) * kw])),
            join3(dot(rot3, wv[:, half * kw : (half + 1) * kw])),
        ], axis=1))

    def packed(product):
        return jnp.concatenate([product[:, :fold], product[:, fold:]], axis=0)

    ax_out[...] = packed(jnp.where(x == 0, both[1], both[0]))
    xa_copy = send(ax_out, ax_in, xa_send, xa_recv, ctx=partner)
    xa_copy.start()
    x_copies[3].start()
    ax_own[...] = packed(jnp.where(x == 0, both[0], both[1]))

    for c in range(2):
        x_copies[c].wait_recv()

        @pl.when(sends(1))
        def _(c=c):
            z_copy(1, c, other, start)

    def to_pairs(src, dst, send_sem, recv_sem):
        def copy(k, receive):
            slot = lax.rem(pair - k + npair, npair) if receive else pair
            return send(
                src, dst.at[slot], send_sem.at[k - 1], recv_sem.at[slot],
                ctx=lax.rem(me + 2 * k, n),
            )
        return copy

    st_copy.wait_recv()
    sz_out[...] = jnp.concatenate(split2(st_out[...] + st_in[...]), axis=0)
    sz_copy = to_pairs(sz_out, sz_all, sz_send, sz_recv)
    for k in range(1, npair):
        sz_copy(k, False).start()
    sz_all[pair] = sz_out[...]

    blocks = span // BLK
    docs = [doc_ref[pair * blocks + b] for b in range(blocks)]

    def count(i, carry):
        one = doc_ref[i]
        return tuple(s + jnp.where(one < d, BLK, 0) for s, d in zip(carry, docs))

    starts = lax.fori_loop(0, doc_ref.shape[0], count, (jnp.int32(0),) * blocks)
    starts = [s - pair * span for s in starts]

    def start_of(position):
        out = jnp.zeros(position.shape, jnp.int32) + starts[0]
        for b in range(1, blocks):
            out = jnp.where(position >= b * BLK, starts[b], out)
        return out

    row = lax.broadcasted_iota(jnp.int32, (span, span), 0)
    key = lax.broadcasted_iota(jnp.int32, (span, span), 1)
    row_start = start_of(row)
    lane_pos = lax.broadcasted_iota(jnp.int32, (1, npos), 1)
    pick_rel = lane_pos // POS_DEV * tokens + pos_ref[...] - pair * span
    token = lax.broadcasted_iota(jnp.int32, (span, npos), 0)

    def one_hot(j):
        return jnp.where(token - j * span == pick_rel, 1.0, 0.0).astype(BF16)

    hot = one_hot(0)
    my_picks = pl.ds(pl.multiple_of(pair * mine, mine), mine)
    pp[...] = dot_tn(hot, lax.broadcasted_iota(jnp.int32, (span, LANES), 0).astype(F32).astype(BF16))
    where_pick = pp[my_picks, :1].astype(jnp.int32)
    where_pick = jnp.concatenate([where_pick, where_pick], axis=0)
    pick_start = start_of(where_pick)

    if hist > 1:
        for c in range(2):
            @pl.when(has(1))
            def _(c=c):
                z_copy(1, c, x, lambda copy: copy.wait_recv())

            @pl.when(jnp.logical_and(has(1), sends(2)))
            def _(c=c):
                z_copy(2, c, x, start)

    for load in loads[:2]:
        load.wait()
    kv[hist, :, :BLK] = jnp.zeros((2, BLK, kw), BF16)
    kp[...] = dot_tn(hot, kv[0, 0])
    vp[...] = dot_tn(hot, kv[0, 1])

    def visit_rows(j):
        rows = span - BLK if j == hist else span
        seen = key[:rows] - j * span >= row_start[:rows]
        if j == 0:
            seen = seen & (key <= row)
        for h in range(2 * kheads):
            at = slice(h // 2 * HD, (h // 2 + 1) * HD)
            keys, values = kv[j, 0, :, at], kv[j, 1, :, at]
            bent = jnp.tanh(
                dot_nt(qb[:rows, h * HD : (h + 1) * HD], keys) * (scale_q / soft_cap)
            )
            weights = jnp.where(seen, jnp.exp(soft_cap * bent), 0.0)
            folded = weights[:, :LANES]
            for a in range(LANES, span, LANES):
                folded = folded + weights[:, a : a + LANES]
            num_new = dot(weights.astype(BF16), values)
            if j == 0:
                zs[h], num[h] = folded, num_new
            else:
                zs[h, :rows] += folded
                num[h, :rows] += num_new

    def visit_picks(j):
        key_at = key[: 2 * mine] - j * span
        seen = (key_at >= pick_start) & (key_at <= where_pick)
        if j > 0:
            hot_j = one_hot(j)
            kp[...] += dot_tn(hot_j, kv[j, 0])
            vp[...] += dot_tn(hot_j, kv[j, 1])
        for h in range(kheads):
            at = slice(h * HD, (h + 1) * HD)
            keys, values = kv[j, 0, :, at], kv[j, 1, :, at]
            bent = jnp.tanh(dot_nt(qp[h], keys) * (scale_q / soft_cap))
            weights = jnp.where(seen, jnp.exp(soft_cap * bent), 0.0)
            folded = weights[:, :LANES]
            for a in range(LANES, span, LANES):
                folded = folded + weights[:, a : a + LANES]
            num_new = dot(weights.astype(BF16), values)
            side = weights * (1.0 - bent * bent)
            sides[h, j] = side
            ms_new = dot(side.astype(BF16), keys)
            if j == 0:
                zp[h], nump[h], ms[h, 2 * mine :] = folded, num_new, ms_new
            else:
                zp[h] += folded
                nump[h] += num_new
                ms[h, 2 * mine :] += ms_new

    def visit_main(j):
        for h in range(kheads):
            at = slice(h * HD, (h + 1) * HD)
            main = (sides[h, j] * dot_nt(gp[h], kv[j, 1, :, at])).astype(BF16)
            ms_new = dot(main, kv[j, 0, :, at])
            if j == 0:
                ms[h, : 2 * mine] = ms_new
            else:
                ms[h, : 2 * mine] += ms_new

    def arrive(j):
        for t in (x, other):
            if j == 1 and hist > 1 and t is x:
                continue
            for c in range(2):
                z_copy(j, c, t, lambda copy: copy.wait_recv())
                if j < hist:
                    @pl.when(sends(j + 1))
                    def _(c=c, t=t):
                        z_copy(j + 1, c, t, start)

    @pl.when(has(1))
    def _():
        arrive(1)

    def pick_rows(picked, src):
        rows_all[:, :qw] = dot_tn(hot, src[...])
        got = rows_all[my_picks, :qw].astype(BF16)
        for h in range(kheads):
            a, b, c = 2 * h * HD, (2 * h + 1) * HD, (2 * h + 2) * HD
            picked[h] = jnp.concatenate([got[:, a:b], got[:, b:c]], axis=0)

    x_copies[2].wait_recv()
    pick_rows(qp, qb)
    visit_rows(0)

    @pl.when(has(1))
    def _():
        visit_rows(1)

    xa_copy.wait_recv()
    az_out[...] = (ax_own[...] + ax_in[...]).astype(BF16)
    az_copy = to_pairs(az_out, az_all, az_send, az_recv)
    for k in range(1, npair):
        az_copy(k, False).start()
    az_all[pair] = jnp.zeros(az_out.shape, BF16)
    ax_own[...] += ax_in[...]

    visit_picks(0)

    @pl.when(has(1))
    def _():
        visit_picks(1)

    x_copies[3].wait_recv()
    pick_rows(gp, gb)
    visit_main(0)

    @pl.when(has(1))
    def _():
        visit_main(1)

    for j in range(2, hist + 1):
        @pl.when(has(j))
        def _(j=j):
            arrive(j)
            visit_rows(j)
            visit_picks(j)
            visit_main(j)

    rows_all[:, :qw] = jnp.zeros((npos, qw), F32)
    for h in range(kheads):
        at = slice(h * HD, (h + 1) * HD)
        total = jnp.sum(zp[h], axis=1, keepdims=True)
        delta = jnp.sum(gp[h].astype(F32) * (nump[h] / total), axis=1, keepdims=True)
        main, side = ms[h, : 2 * mine], ms[h, 2 * mine :]
        dq = (scale_q * (main - delta * side) / total).astype(BF16).astype(F32)
        for i in range(2):
            rows_all[my_picks, (2 * h + i) * HD : (2 * h + i + 1) * HD] = dq[
                i * mine : (i + 1) * mine
            ]

    for k in range(1, npair):
        sz_copy(k, True).wait_recv()
    sz = sz_all[0].astype(F32)
    for i in range(1, npair):
        sz = sz + sz_all[i].astype(F32)
    rank_state = sz[:rank, :npos] + sz[rank:, :npos]
    loads[13].wait()
    bias_row = lax.broadcasted_iota(jnp.int32, rank_state.shape, 0)
    for r in range(rank):
        rank_state = rank_state + jnp.where(bias_row == r, bias_ref[r], 0.0)

    s_hi, s_lo = split2(rank_state)
    s_both = jnp.concatenate([s_hi, s_lo], axis=0)
    q_rows = rows_all[:, :qw].astype(BF16)
    q2 = dot(s_both, q_rows)
    term = q2[:rank] + q2[rank:]
    tq_out[...] = jnp.concatenate([term[:, : qw // 2], term[:, qw // 2 :]], axis=0).astype(BF16)

    def to_all(src, dst, send_sem, recv_sem):
        def each(run):
            for d in range(n):
                @pl.when(me != d)
                def _(d=d):
                    run(d)

        def begin():
            each(lambda d: send(
                src, dst.at[me], send_sem.at[d], recv_sem.at[me], ctx=d
            ).start())

        def received():
            each(lambda d: send(
                src, dst.at[d], send_sem.at[d], recv_sem.at[d], ctx=d
            ).wait_recv())

        def gone():
            each(lambda d: send(
                src, dst.at[me], send_sem.at[d], recv_sem.at[me], ctx=d
            ).wait_send())

        return begin, received, gone

    tq_begin, tq_received, tq_gone = to_all(tq_out, tq_all, tq_send, tq_recv)
    tq_begin()
    tq_all[me] = tq_out[...]

    row1 = lax.broadcasted_iota(jnp.int32, (span, npos), 0)
    seen = (pick_rel >= start_of(row1)) & (pick_rel <= row1)
    for h in range(kheads):
        at = slice(h * HD, (h + 1) * HD)
        keys = kp[:, at].astype(BF16)
        values = vp[:, at].astype(BF16)
        dk = dv = 0.0
        for i in range(2 * h, 2 * h + 2):
            query = qb[:, i * HD : (i + 1) * HD]
            grad = gb[:, i * HD : (i + 1) * HD]
            total = jnp.sum(zs[i], axis=1, keepdims=True)
            delta = jnp.sum(grad.astype(F32) * (num[i] / total), axis=1, keepdims=True)
            bent = jnp.tanh(dot_nt(query, keys) * (scale_q / soft_cap))
            prob = jnp.where(seen, jnp.exp(soft_cap * bent), 0.0) / total
            dscore = prob * (dot_nt(grad, values) - delta) * (1.0 - bent * bent)
            dv = dv + dot_tn(prob.astype(BF16), grad)
            dk = dk + dot_tn(dscore.astype(BF16), query)
        rows_all[:, qw + h * HD : qw + (h + 1) * HD] = scale_q * dk
        rows_all[:, qw + kw + h * HD : qw + kw + (h + 1) * HD] = dv

    r_hi, r_lo = split2(rows_all[:, qw:])
    k2 = dot(s_both, r_hi)
    term = k2[:rank] + k2[rank:] + dot(s_hi, r_lo)
    t_out[...] = jnp.concatenate([term[:, :kw], term[:, kw:]], axis=0).astype(BF16)
    t_begin, t_received, t_gone = to_all(t_out, t_all, t_send, t_recv)
    t_begin()
    t_all[me] = t_out[...]

    rank_up = join3(dot_nt(rot3, up))
    first_core = jnp.where(core == 0, 1.0, 0.0)
    for k in range(1, npair):
        az_copy(k, True).wait_recv()
    az = ax_own[...] + az_all[0].astype(F32)
    for i in range(1, npair):
        az = az + az_all[i].astype(F32)
    rw = jnp.concatenate([az[:rank], az[rank:]], axis=1)
    a_hi, a_lo = split2(rw)
    a_both = jnp.concatenate([a_hi, a_lo], axis=0)
    a2 = dot_nt(a_both[:, :qw], q_rows) + dot_nt(a_both[:, qw:], r_hi)
    rg = a2[:rank] + a2[rank:] + dot_nt(a_hi[:, qw:], r_lo) + first_core * rank_up
    if lanes > npos:
        rg_out[...] = jnp.zeros(rg_out.shape, F32)
    rg_out[:, :npos] = rg
    rg_begin, rg_received, rg_gone = to_all(rg_out, rg_all, rg_send, rg_recv)
    rg_begin()
    rg_all[me] = rg_out[...]
    rot_up = first_core * join3(dot(split3(rank_state), up))

    def sum_over_pairs(ref):
        sums = []
        for i in range(2):
            total = ref[i].astype(F32)
            for z in range(1, npair):
                total = total + ref[2 * z + i].astype(F32)
            sums.append(total)
        return sums

    def weighted(w, parts):
        return dot_nt(w[...], jnp.concatenate(split2(jnp.concatenate(parts, axis=1)), axis=0))

    tq_received()
    res = weighted(
        wq, [p for s in sum_over_pairs(tq_all) for p in (s[:rank], s[rank:])]
    )
    t_received()
    sums = sum_over_pairs(t_all)
    res = res + weighted(wk, [s[:rank, :kw] for s in sums])
    res = res + weighted(wv, [s[rank:, :kw] for s in sums])
    res = jnp.transpose(res)
    grad = res[:rank] + res[rank:] + rot_up
    rg_received()
    rg = rg_all[0]
    for i in range(1, n):
        rg = rg + rg_all[i]
    rg = rg[:, :npos]
    grad_proj = join3(dot(split3(rg), hidden))

    width = hidden.shape[1]
    room = sw_out.shape[2]
    if room > width:
        sw_out[0] = jnp.zeros((rank, room), F32)
        sw_out[1] = jnp.zeros((rank, room), F32)
    sw_out[0, :, :width] = grad - grad_proj
    sw_out[1, :, :width] = grad_proj
    sw_out[2, :, :lanes] = jnp.broadcast_to(jnp.sum(rg, axis=1, keepdims=True), (rank, lanes))
    sw_copy = send(sw_out, sw_in, sw_send, sw_recv, head=1 - core)
    sw_copy.start()
    sw_copy.wait_recv()
    rot_out[...] = sw_out[0, :, :width] + sw_in[0, :, :width]
    proj_out[...] = sw_out[1, :, :width] + sw_in[1, :, :width]
    bias = sw_out[2, :, :lanes] + sw_in[2, :, :lanes]
    for r in range(rank):
        bias_out[r] = bias[r, 0]

    sw_copy.wait_send()
    xa_copy.wait_send()
    for copy in x_copies:
        copy.wait_send()
    for k in range(1, npair):
        az_copy(k, False).wait_send()
        sz_copy(k, False).wait_send()
    st_copy.wait_send()
    rg_gone()
    tq_gone()
    t_gone()

    def sent(copy):
        copy.wait_send()

    for j in range(1, hist + 1):
        @pl.when(sends(j))
        def _(j=j):
            for c in range(2):
                z_copy(j, c, x, sent, first=j == 1)
                z_copy(j, c, other, sent)


def finish(rot_in, proj_in, bias_in, rot_out, proj_out, bias_out):
    rot_out[...] = rot_in[...]
    proj_out[...] = proj_in[...]
    bias_out[...] = bias_in[...]


def local(n, *args):
    args = list(args)
    args[5] = args[5].reshape(1, -1)
    queries, key_states = args[0], args[1]
    hidden, rotation = args[6], args[11]
    tokens, q_width = queries.shape
    kv_width = key_states.shape[1]
    qw, kw = q_width // 2, kv_width // 2
    kheads = kw // HD
    width = hidden.shape[1]
    rank = rotation.shape[0]
    npair = n // 2
    hist = npair // 2
    npos = n * POS_DEV
    mine = 2 * POS_DEV
    lanes = round_up(npos, LANES)
    span = 2 * tokens
    wide = qw + 2 * kw
    fold = wide // 2
    room = max(round_up(width, LANES), lanes)
    vmem = pl.BlockSpec(memory_space=pltpu.VMEM)
    smem = pl.BlockSpec(memory_space=pltpu.SMEM)
    hbm = pl.BlockSpec(memory_space=pltpu.HBM)
    dma = pltpu.SemaphoreType.DMA
    outs = pl.pallas_call(
        functools.partial(kernel, n),
        out_shape=(
            jax.ShapeDtypeStruct((rank, width), F32),
            jax.ShapeDtypeStruct((rank, width), F32),
            jax.ShapeDtypeStruct((rank,), F32),
        ),
        in_specs=[hbm] * len(args),
        out_specs=(vmem, vmem, smem),
        scratch_shapes=[
            pltpu.VMEM((hist + 1, 2, span, kw), BF16),
            pltpu.VMEM((span, qw), BF16),
            pltpu.VMEM((span, qw), BF16),
            pltpu.VMEM((kheads, 2 * mine, HD), BF16),
            pltpu.VMEM((kheads, 2 * mine, HD), BF16),
            pltpu.VMEM((npos, LANES), F32),
            pltpu.VMEM((2 * kheads, span, LANES), F32),
            pltpu.VMEM((2 * kheads, span, HD), F32),
            pltpu.VMEM((kheads, 2 * mine, LANES), F32),
            pltpu.VMEM((kheads, 2 * mine, HD), F32),
            pltpu.VMEM((kheads, 4 * mine, HD), F32),
            pltpu.VMEM((kheads, hist + 1, 2 * mine, span), F32),
            pltpu.VMEM((npos, kw), F32),
            pltpu.VMEM((npos, kw), F32),
            pltpu.VMEM((npos, wide), F32),
            pltpu.VMEM((2 * rank, fold), F32),
            pltpu.VMEM((2 * rank, fold), F32),
            pltpu.VMEM((2 * rank, fold), F32),
            pltpu.VMEM((2 * rank, fold), BF16),
            pltpu.VMEM((npair, 2 * rank, fold), BF16),
            pltpu.VMEM((2 * rank, qw // 2), BF16),
            pltpu.VMEM((n, 2 * rank, qw // 2), BF16),
            pltpu.VMEM((2 * rank, kw), BF16),
            pltpu.VMEM((n, 2 * rank, kw), BF16),
            pltpu.VMEM((3, rank, room), F32),
            pltpu.VMEM((3, rank, room), F32),
            pltpu.VMEM((rank, lanes), F32),
            pltpu.VMEM((rank, lanes), F32),
            pltpu.VMEM((2 * rank, lanes), BF16),
            pltpu.VMEM((npair, 2 * rank, lanes), BF16),
            pltpu.VMEM((rank, lanes), F32),
            pltpu.VMEM((n, rank, lanes), F32),
            pltpu.VMEM((width, q_width), BF16),
            pltpu.VMEM((width, kv_width), BF16),
            pltpu.VMEM((width, kv_width), BF16),
            pltpu.SMEM(args[4].shape, jnp.int32),
            pltpu.VMEM(args[5].shape, jnp.int32),
            pltpu.VMEM(hidden.shape, BF16),
            pltpu.VMEM(hidden.shape, BF16),
            pltpu.VMEM(rotation.shape, F32),
            pltpu.VMEM(rotation.shape, F32),
            pltpu.SMEM((rank,), F32),
            dma((len(args),)),
            dma((hist, 2, 2)), dma((hist, 2, 2)),
            dma((4,)), dma((4,)),
            dma, dma,
            dma((npair,)), dma((npair,)),
            dma((n,)), dma((n,)),
            dma((n,)), dma((n,)),
            dma, dma,
            dma, dma,
            dma((npair,)), dma((npair,)),
            dma((n,)), dma((n,)),
        ],
        compiler_params=pltpu.CompilerParams(
            collective_id=0, has_side_effects=True, vmem_limit_bytes=64 << 20
        ),
        name="rank_backward",
    )(*args)
    return pl.pallas_call(
        finish,
        out_shape=tuple(jax.ShapeDtypeStruct(out.shape, out.dtype) for out in outs),
        in_specs=[vmem] * 3,
        out_specs=(vmem,) * 3,
        name="finish",
    )(*outs)


def solution(mesh):
    in_specs = (
        P(("groups", "ctx"), "head"),
        P(("groups", "ctx"), "head"),
        P(("groups", "ctx"), "head"),
        P(("groups", "ctx"), "head"),
        P("groups"),
        P("groups"),
        P("groups", "ctx"),
        P("groups", "ctx"),
        P("ctx", "head"),
        P("ctx", "head"),
        P("ctx", "head"),
        P(None, "ctx"),
        P(None, "ctx"),
        P(),
    )
    out_specs = (P("groups", "ctx"), P("groups", "ctx"), P("groups"))
    return jax.shard_map(
        functools.partial(local, mesh.shape["ctx"]),
        mesh=mesh, in_specs=in_specs, out_specs=out_specs, check_vma=False,
    )
```

```python
import functools

import jax
import jax.numpy as jnp
from jax import lax
from jax.experimental import pallas as pl
from jax.experimental.pallas import tpu as pltpu
from jax.sharding import PartitionSpec as P

HD = 128
BLK = 64
POS_DEV = 8
LANES = 128

scale_q = 1.0 / 12.0
soft_cap = 50.0

MESH = pl.DeviceIdType.MESH
F32 = jnp.float32
BF16 = jnp.bfloat16


def round_up(value, multiple):
    return (value + multiple - 1) // multiple * multiple


def dot(left, right):
    return jnp.dot(left, right, preferred_element_type=F32)


def dot_nt(left, right):
    return lax.dot_general(left, right, (((1,), (1,)), ((), ())), preferred_element_type=F32)


def dot_tn(left, right):
    return lax.dot_general(left, right, (((0,), (0,)), ((), ())), preferred_element_type=F32)


def split2(x):
    hi = x.astype(BF16)
    return hi, (x - hi.astype(F32)).astype(BF16)


def split3(x):
    hi = x.astype(BF16)
    rest = x - hi.astype(F32)
    mid = rest.astype(BF16)
    low = (rest - mid.astype(F32)).astype(BF16)
    return jnp.concatenate([hi, mid, low], axis=0)


def join3(x):
    r = x.shape[0] // 3
    return x[:r] + x[r : 2 * r] + x[2 * r :]


def kernel(
    n,
    q_hbm, k_hbm, v_hbm, g_hbm, doc_hbm, pos_hbm, hidden_hbm, up_hbm,
    wq_hbm, wk_hbm, wv_hbm, rot_hbm, proj_hbm, bias_hbm,
    rot_out, proj_out, bias_out,
    kv, qb, gb, qp, gp, pp, zs, num, zp, nump, ms, sides, kp, vp, rows_all,
    ax_out, ax_own, ax_in, az_out, az_all, tq_out, tq_all, t_out, t_all, sw_out, sw_in,
    st_out, st_in, sz_out, sz_all, rg_out, rg_all,
    wq, wk, wv, doc_ref, pos_ref, hidden_ref, up_ref, rot_ref, proj_ref, bias_ref,
    l_sem, z_send, z_recv, x_send, x_recv, xa_send, xa_recv, az_send, az_recv,
    tq_send, tq_recv, t_send, t_recv, sw_send, sw_recv,
    st_send, st_recv, sz_send, sz_recv, rg_send, rg_recv,
):
    me = lax.axis_index("ctx")
    core = lax.axis_index("head")
    pair = me // 2
    x = lax.rem(me, 2)
    partner = me + 1 - 2 * x
    npair = n // 2
    hist = npair // 2
    tokens = q_hbm.shape[0]
    span = 2 * tokens
    kw = kv.shape[3]
    qw = qb.shape[1]
    kheads = kw // HD
    npos = n * POS_DEV
    mine = 2 * POS_DEV
    lanes = round_up(npos, LANES)
    wide = qw + 2 * kw
    fold = wide // 2

    barrier = pltpu.get_barrier_semaphore()
    for k in range(1, n):
        pl.semaphore_signal(
            barrier, inc=1, device_id={"ctx": lax.rem(me + k, n)}, device_id_type=MESH
        )
    pl.semaphore_signal(barrier, inc=1, device_id={"head": 1 - core}, device_id_type=MESH)

    own_rows = pl.ds(pl.multiple_of(x * tokens, tokens), tokens)

    def cols(ref, which, width):
        return ref.at[:, pl.ds(pl.multiple_of(which * width, width), width)]

    pairs_in = (
        (cols(k_hbm, x, kw), kv.at[0, 0, own_rows]), (cols(v_hbm, x, kw), kv.at[0, 1, own_rows]),
        (doc_hbm, doc_ref), (pos_hbm, pos_ref),
        (cols(q_hbm, x, qw), qb.at[own_rows]), (cols(g_hbm, x, qw), gb.at[own_rows]),
        (rot_hbm, rot_ref), (proj_hbm, proj_ref), (hidden_hbm, hidden_ref),
        (wq_hbm, wq), (wk_hbm, wk), (wv_hbm, wv), (up_hbm, up_ref), (bias_hbm, bias_ref),
    )
    loads = [
        pltpu.make_async_copy(src, dst, l_sem.at[i]) for i, (src, dst) in enumerate(pairs_in)
    ]
    for load in loads:
        load.start()

    def send(src, dst, send_sem, recv_sem, **where):
        return pltpu.make_async_remote_copy(
            src_ref=src, dst_ref=dst, send_sem=send_sem, recv_sem=recv_sem,
            device_id=where, device_id_type=MESH,
        )

    above = lax.rem(me + 2, n)

    def z_copy(j, c, t, run, first=False):
        def go(start, size):
            rows = pl.ds(start, size)
            src = kv.at[j - 1, c, rows]
            if first:
                src = cols((k_hbm, v_hbm)[c], x, kw)
                if size < tokens:
                    src = src.at[pl.ds(tokens - size, size)]
            run(send(src, kv.at[j, c, rows], z_send.at[j - 1, c, t], z_recv.at[j - 1, c, t],
                     ctx=above))
        if j < hist:
            go(pl.multiple_of(t * tokens, tokens), tokens)
        else:
            @pl.when(t == 0)
            def _():
                go(BLK, tokens - BLK)

            @pl.when(t == 1)
            def _():
                go(tokens, tokens)

    def start(copy):
        copy.start()

    def has(j):
        return pair >= j

    def sends(j):
        return jnp.logical_and(pair >= j - 1, pair + 1 < npair)

    other = 1 - x
    x_copies = [
        send(cols(k_hbm, other, kw), kv.at[0, 0, own_rows], x_send.at[0], x_recv.at[0], ctx=partner),
        send(cols(v_hbm, other, kw), kv.at[0, 1, own_rows], x_send.at[1], x_recv.at[1], ctx=partner),
        send(cols(q_hbm, other, qw), qb.at[own_rows], x_send.at[2], x_recv.at[2], ctx=partner),
        send(cols(g_hbm, other, qw), gb.at[own_rows], x_send.at[3], x_recv.at[3], ctx=partner),
    ]

    pl.semaphore_wait(barrier, n)
    for copy in x_copies[:2]:
        copy.start()

    @pl.when(sends(1))
    def _():
        for c in range(2):
            z_copy(1, c, x, start, first=True)

    for load in loads[2:9]:
        load.wait()
    rot = rot_ref[...]
    rank = rot.shape[0]
    rot3 = split3(rot)
    hidden = hidden_ref[...]
    if lanes > npos:
        st_out[...] = jnp.zeros(st_out.shape, F32)
    st_out[:, :npos] = join3(dot_nt(split3(proj_ref[...] - rot), hidden))
    st_copy = send(st_out, st_in, st_send, st_recv, ctx=partner)
    st_copy.start()
    x_copies[2].start()
    for load in loads[9:13]:
        load.wait()
    up = up_ref[...]
    both = []
    for half in range(2):
        both.append(jnp.concatenate([
            join3(dot(rot3, wq[:, half * qw : (half + 1) * qw])),
            join3(dot(rot3, wk[:, half * kw : (half + 1) * kw])),
            join3(dot(rot3, wv[:, half * kw : (half + 1) * kw])),
        ], axis=1))

    def packed(product):
        return jnp.concatenate([product[:, :fold], product[:, fold:]], axis=0)

    ax_out[...] = packed(jnp.where(x == 0, both[1], both[0]))
    xa_copy = send(ax_out, ax_in, xa_send, xa_recv, ctx=partner)
    xa_copy.start()
    x_copies[3].start()
    ax_own[...] = packed(jnp.where(x == 0, both[0], both[1]))

    for c in range(2):
        x_copies[c].wait_recv()

        @pl.when(sends(1))
        def _(c=c):
            z_copy(1, c, other, start)

    def to_pairs(src, dst, send_sem, recv_sem):
        def copy(k, receive):
            slot = lax.rem(pair - k + npair, npair) if receive else pair
            return send(
                src, dst.at[slot], send_sem.at[k - 1], recv_sem.at[slot],
                ctx=lax.rem(me + 2 * k, n),
            )
        return copy

    st_copy.wait_recv()
    sz_out[...] = jnp.concatenate(split2(st_out[...] + st_in[...]), axis=0)
    sz_copy = to_pairs(sz_out, sz_all, sz_send, sz_recv)
    for k in range(1, npair):
        sz_copy(k, False).start()
    sz_all[pair] = sz_out[...]

    blocks = span // BLK
    docs = [doc_ref[pair * blocks + b] for b in range(blocks)]

    def count(i, carry):
        one = doc_ref[i]
        return tuple(s + jnp.where(one < d, BLK, 0) for s, d in zip(carry, docs))

    starts = lax.fori_loop(0, doc_ref.shape[0], count, (jnp.int32(0),) * blocks)
    starts = [s - pair * span for s in starts]

    def start_of(position):
        out = jnp.zeros(position.shape, jnp.int32) + starts[0]
        for b in range(1, blocks):
            out = jnp.where(position >= b * BLK, starts[b], out)
        return out

    row = lax.broadcasted_iota(jnp.int32, (span, span), 0)
    key = lax.broadcasted_iota(jnp.int32, (span, span), 1)
    row_start = start_of(row)
    lane_pos = lax.broadcasted_iota(jnp.int32, (1, npos), 1)
    pick_rel = lane_pos // POS_DEV * tokens + pos_ref[...] - pair * span
    token = lax.broadcasted_iota(jnp.int32, (span, npos), 0)

    def one_hot(j):
        return jnp.where(token - j * span == pick_rel, 1.0, 0.0).astype(BF16)

    hot = one_hot(0)
    my_picks = pl.ds(pl.multiple_of(pair * mine, mine), mine)
    pp[...] = dot_tn(hot, lax.broadcasted_iota(jnp.int32, (span, LANES), 0).astype(F32).astype(BF16))
    where_pick = pp[my_picks, :1].astype(jnp.int32)
    where_pick = jnp.concatenate([where_pick, where_pick], axis=0)
    pick_start = start_of(where_pick)

    if hist > 1:
        for c in range(2):
            @pl.when(has(1))
            def _(c=c):
                z_copy(1, c, x, lambda copy: copy.wait_recv())

            @pl.when(jnp.logical_and(has(1), sends(2)))
            def _(c=c):
                z_copy(2, c, x, start)

    for load in loads[:2]:
        load.wait()
    kv[hist, :, :BLK] = jnp.zeros((2, BLK, kw), BF16)
    kp[...] = dot_tn(hot, kv[0, 0])
    vp[...] = dot_tn(hot, kv[0, 1])

    def visit_rows(j):
        rows = span - BLK if j == hist else span
        seen = key[:rows] - j * span >= row_start[:rows]
        if j == 0:
            seen = seen & (key <= row)
        for h in range(2 * kheads):
            at = slice(h // 2 * HD, (h // 2 + 1) * HD)
            keys, values = kv[j, 0, :, at], kv[j, 1, :, at]
            bent = jnp.tanh(
                dot_nt(qb[:rows, h * HD : (h + 1) * HD], keys) * (scale_q / soft_cap)
            )
            weights = jnp.where(seen, jnp.exp(soft_cap * bent), 0.0)
            folded = weights[:, :LANES]
            for a in range(LANES, span, LANES):
                folded = folded + weights[:, a : a + LANES]
            num_new = dot(weights.astype(BF16), values)
            if j == 0:
                zs[h], num[h] = folded, num_new
            else:
                zs[h, :rows] += folded
                num[h, :rows] += num_new

    def visit_picks(j):
        key_at = key[: 2 * mine] - j * span
        seen = (key_at >= pick_start) & (key_at <= where_pick)
        if j > 0:
            hot_j = one_hot(j)
            kp[...] += dot_tn(hot_j, kv[j, 0])
            vp[...] += dot_tn(hot_j, kv[j, 1])
        for h in range(kheads):
            at = slice(h * HD, (h + 1) * HD)
            keys, values = kv[j, 0, :, at], kv[j, 1, :, at]
            bent = jnp.tanh(dot_nt(qp[h], keys) * (scale_q / soft_cap))
            weights = jnp.where(seen, jnp.exp(soft_cap * bent), 0.0)
            folded = weights[:, :LANES]
            for a in range(LANES, span, LANES):
                folded = folded + weights[:, a : a + LANES]
            num_new = dot(weights.astype(BF16), values)
            side = weights * (1.0 - bent * bent)
            sides[h, j] = side
            ms_new = dot(side.astype(BF16), keys)
            if j == 0:
                zp[h], nump[h], ms[h, 2 * mine :] = folded, num_new, ms_new
            else:
                zp[h] += folded
                nump[h] += num_new
                ms[h, 2 * mine :] += ms_new

    def visit_main(j):
        for h in range(kheads):
            at = slice(h * HD, (h + 1) * HD)
            main = (sides[h, j] * dot_nt(gp[h], kv[j, 1, :, at])).astype(BF16)
            ms_new = dot(main, kv[j, 0, :, at])
            if j == 0:
                ms[h, : 2 * mine] = ms_new
            else:
                ms[h, : 2 * mine] += ms_new

    def arrive(j):
        for t in (x, other):
            if j == 1 and hist > 1 and t is x:
                continue
            for c in range(2):
                z_copy(j, c, t, lambda copy: copy.wait_recv())
                if j < hist:
                    @pl.when(sends(j + 1))
                    def _(c=c, t=t):
                        z_copy(j + 1, c, t, start)

    @pl.when(has(1))
    def _():
        arrive(1)

    def pick_rows(picked, src):
        rows_all[:, :qw] = dot_tn(hot, src[...])
        got = rows_all[my_picks, :qw].astype(BF16)
        for h in range(kheads):
            a, b, c = 2 * h * HD, (2 * h + 1) * HD, (2 * h + 2) * HD
            picked[h] = jnp.concatenate([got[:, a:b], got[:, b:c]], axis=0)

    x_copies[2].wait_recv()
    pick_rows(qp, qb)
    xa_copy.wait_recv()
    az_out[...] = (ax_own[...] + ax_in[...]).astype(BF16)
    az_copy = to_pairs(az_out, az_all, az_send, az_recv)
    for k in range(1, npair):
        az_copy(k, False).start()
    az_all[pair] = jnp.zeros(az_out.shape, BF16)
    ax_own[...] += ax_in[...]

    visit_rows(0)

    @pl.when(has(1))
    def _():
        visit_rows(1)

    visit_picks(0)

    @pl.when(has(1))
    def _():
        visit_picks(1)

    x_copies[3].wait_recv()
    pick_rows(gp, gb)
    visit_main(0)

    @pl.when(has(1))
    def _():
        visit_main(1)

    for j in range(2, hist + 1):
        @pl.when(has(j))
        def _(j=j):
            arrive(j)
            visit_rows(j)
            visit_picks(j)
            visit_main(j)

    rows_all[:, :qw] = jnp.zeros((npos, qw), F32)
    for h in range(kheads):
        at = slice(h * HD, (h + 1) * HD)
        total = jnp.sum(zp[h], axis=1, keepdims=True)
        delta = jnp.sum(gp[h].astype(F32) * (nump[h] / total), axis=1, keepdims=True)
        main, side = ms[h, : 2 * mine], ms[h, 2 * mine :]
        dq = (scale_q * (main - delta * side) / total).astype(BF16).astype(F32)
        for i in range(2):
            rows_all[my_picks, (2 * h + i) * HD : (2 * h + i + 1) * HD] = dq[
                i * mine : (i + 1) * mine
            ]

    for k in range(1, npair):
        sz_copy(k, True).wait_recv()
    sz = sz_all[0].astype(F32)
    for i in range(1, npair):
        sz = sz + sz_all[i].astype(F32)
    rank_state = sz[:rank, :npos] + sz[rank:, :npos]
    loads[13].wait()
    bias_row = lax.broadcasted_iota(jnp.int32, rank_state.shape, 0)
    for r in range(rank):
        rank_state = rank_state + jnp.where(bias_row == r, bias_ref[r], 0.0)

    s_hi, s_lo = split2(rank_state)
    s_both = jnp.concatenate([s_hi, s_lo], axis=0)
    q_rows = rows_all[:, :qw].astype(BF16)
    q2 = dot(s_both, q_rows)
    term = q2[:rank] + q2[rank:]
    tq_out[...] = jnp.concatenate([term[:, : qw // 2], term[:, qw // 2 :]], axis=0).astype(BF16)

    def to_all(src, dst, send_sem, recv_sem):
        def each(run):
            for d in range(n):
                @pl.when(me != d)
                def _(d=d):
                    run(d)

        def begin():
            each(lambda d: send(
                src, dst.at[me], send_sem.at[d], recv_sem.at[me], ctx=d
            ).start())

        def received():
            each(lambda d: send(
                src, dst.at[d], send_sem.at[d], recv_sem.at[d], ctx=d
            ).wait_recv())

        def gone():
            each(lambda d: send(
                src, dst.at[me], send_sem.at[d], recv_sem.at[me], ctx=d
            ).wait_send())

        return begin, received, gone

    tq_begin, tq_received, tq_gone = to_all(tq_out, tq_all, tq_send, tq_recv)
    tq_begin()
    tq_all[me] = tq_out[...]

    row1 = lax.broadcasted_iota(jnp.int32, (span, npos), 0)
    seen = (pick_rel >= start_of(row1)) & (pick_rel <= row1)
    for h in range(kheads):
        at = slice(h * HD, (h + 1) * HD)
        keys = kp[:, at].astype(BF16)
        values = vp[:, at].astype(BF16)
        dk = dv = 0.0
        for i in range(2 * h, 2 * h + 2):
            query = qb[:, i * HD : (i + 1) * HD]
            grad = gb[:, i * HD : (i + 1) * HD]
            total = jnp.sum(zs[i], axis=1, keepdims=True)
            delta = jnp.sum(grad.astype(F32) * (num[i] / total), axis=1, keepdims=True)
            bent = jnp.tanh(dot_nt(query, keys) * (scale_q / soft_cap))
            prob = jnp.where(seen, jnp.exp(soft_cap * bent), 0.0) / total
            dscore = prob * (dot_nt(grad, values) - delta) * (1.0 - bent * bent)
            dv = dv + dot_tn(prob.astype(BF16), grad)
            dk = dk + dot_tn(dscore.astype(BF16), query)
        rows_all[:, qw + h * HD : qw + (h + 1) * HD] = scale_q * dk
        rows_all[:, qw + kw + h * HD : qw + kw + (h + 1) * HD] = dv

    r_hi, r_lo = split2(rows_all[:, qw:])
    k2 = dot(s_both, r_hi)
    term = k2[:rank] + k2[rank:] + dot(s_hi, r_lo)
    t_out[...] = jnp.concatenate([term[:, :kw], term[:, kw:]], axis=0).astype(BF16)
    t_begin, t_received, t_gone = to_all(t_out, t_all, t_send, t_recv)
    t_begin()
    t_all[me] = t_out[...]

    rank_up = join3(dot_nt(rot3, up))
    first_core = jnp.where(core == 0, 1.0, 0.0)
    for k in range(1, npair):
        az_copy(k, True).wait_recv()
    az = ax_own[...] + az_all[0].astype(F32)
    for i in range(1, npair):
        az = az + az_all[i].astype(F32)
    rw = jnp.concatenate([az[:rank], az[rank:]], axis=1)
    a_hi, a_lo = split2(rw)
    a_both = jnp.concatenate([a_hi, a_lo], axis=0)
    a2 = dot_nt(a_both[:, :qw], q_rows) + dot_nt(a_both[:, qw:], r_hi)
    rg = a2[:rank] + a2[rank:] + dot_nt(a_hi[:, qw:], r_lo) + first_core * rank_up
    if lanes > npos:
        rg_out[...] = jnp.zeros(rg_out.shape, F32)
    rg_out[:, :npos] = rg
    rg_begin, rg_received, rg_gone = to_all(rg_out, rg_all, rg_send, rg_recv)
    rg_begin()
    rg_all[me] = rg_out[...]
    rot_up = first_core * join3(dot(split3(rank_state), up))

    def sum_over_pairs(ref):
        sums = []
        for i in range(2):
            total = ref[i].astype(F32)
            for z in range(1, npair):
                total = total + ref[2 * z + i].astype(F32)
            sums.append(total)
        return sums

    def weighted(w, parts):
        return dot_nt(w[...], jnp.concatenate(split2(jnp.concatenate(parts, axis=1)), axis=0))

    tq_received()
    res = weighted(
        wq, [p for s in sum_over_pairs(tq_all) for p in (s[:rank], s[rank:])]
    )
    t_received()
    sums = sum_over_pairs(t_all)
    res = res + weighted(wk, [s[:rank, :kw] for s in sums])
    res = res + weighted(wv, [s[rank:, :kw] for s in sums])
    res = jnp.transpose(res)
    grad = res[:rank] + res[rank:] + rot_up
    rg_received()
    rg = rg_all[0]
    for i in range(1, n):
        rg = rg + rg_all[i]
    rg = rg[:, :npos]
    grad_proj = join3(dot(split3(rg), hidden))

    width = hidden.shape[1]
    room = sw_out.shape[2]
    if room > width:
        sw_out[0] = jnp.zeros((rank, room), F32)
        sw_out[1] = jnp.zeros((rank, room), F32)
    sw_out[0, :, :width] = grad - grad_proj
    sw_out[1, :, :width] = grad_proj
    sw_out[2, :, :lanes] = jnp.broadcast_to(jnp.sum(rg, axis=1, keepdims=True), (rank, lanes))
    sw_copy = send(sw_out, sw_in, sw_send, sw_recv, head=1 - core)
    sw_copy.start()
    sw_copy.wait_recv()
    rot_out[...] = sw_out[0, :, :width] + sw_in[0, :, :width]
    proj_out[...] = sw_out[1, :, :width] + sw_in[1, :, :width]
    bias = sw_out[2, :, :lanes] + sw_in[2, :, :lanes]
    for r in range(rank):
        bias_out[r] = bias[r, 0]

    sw_copy.wait_send()
    xa_copy.wait_send()
    for copy in x_copies:
        copy.wait_send()
    for k in range(1, npair):
        az_copy(k, False).wait_send()
        sz_copy(k, False).wait_send()
    st_copy.wait_send()
    rg_gone()
    tq_gone()
    t_gone()

    def sent(copy):
        copy.wait_send()

    for j in range(1, hist + 1):
        @pl.when(sends(j))
        def _(j=j):
            for c in range(2):
                z_copy(j, c, x, sent, first=j == 1)
                z_copy(j, c, other, sent)


def finish(rot_in, proj_in, bias_in, rot_out, proj_out, bias_out):
    rot_out[...] = rot_in[...]
    proj_out[...] = proj_in[...]
    bias_out[...] = bias_in[...]


def local(n, *args):
    args = list(args)
    args[5] = args[5].reshape(1, -1)
    queries, key_states = args[0], args[1]
    hidden, rotation = args[6], args[11]
    tokens, q_width = queries.shape
    kv_width = key_states.shape[1]
    qw, kw = q_width // 2, kv_width // 2
    kheads = kw // HD
    width = hidden.shape[1]
    rank = rotation.shape[0]
    npair = n // 2
    hist = npair // 2
    npos = n * POS_DEV
    mine = 2 * POS_DEV
    lanes = round_up(npos, LANES)
    span = 2 * tokens
    wide = qw + 2 * kw
    fold = wide // 2
    room = max(round_up(width, LANES), lanes)
    vmem = pl.BlockSpec(memory_space=pltpu.VMEM)
    smem = pl.BlockSpec(memory_space=pltpu.SMEM)
    hbm = pl.BlockSpec(memory_space=pltpu.HBM)
    dma = pltpu.SemaphoreType.DMA
    outs = pl.pallas_call(
        functools.partial(kernel, n),
        out_shape=(
            jax.ShapeDtypeStruct((rank, width), F32),
            jax.ShapeDtypeStruct((rank, width), F32),
            jax.ShapeDtypeStruct((rank,), F32),
        ),
        in_specs=[hbm] * len(args),
        out_specs=(vmem, vmem, smem),
        scratch_shapes=[
            pltpu.VMEM((hist + 1, 2, span, kw), BF16),
            pltpu.VMEM((span, qw), BF16),
            pltpu.VMEM((span, qw), BF16),
            pltpu.VMEM((kheads, 2 * mine, HD), BF16),
            pltpu.VMEM((kheads, 2 * mine, HD), BF16),
            pltpu.VMEM((npos, LANES), F32),
            pltpu.VMEM((2 * kheads, span, LANES), F32),
            pltpu.VMEM((2 * kheads, span, HD), F32),
            pltpu.VMEM((kheads, 2 * mine, LANES), F32),
            pltpu.VMEM((kheads, 2 * mine, HD), F32),
            pltpu.VMEM((kheads, 4 * mine, HD), F32),
            pltpu.VMEM((kheads, hist + 1, 2 * mine, span), F32),
            pltpu.VMEM((npos, kw), F32),
            pltpu.VMEM((npos, kw), F32),
            pltpu.VMEM((npos, wide), F32),
            pltpu.VMEM((2 * rank, fold), F32),
            pltpu.VMEM((2 * rank, fold), F32),
            pltpu.VMEM((2 * rank, fold), F32),
            pltpu.VMEM((2 * rank, fold), BF16),
            pltpu.VMEM((npair, 2 * rank, fold), BF16),
            pltpu.VMEM((2 * rank, qw // 2), BF16),
            pltpu.VMEM((n, 2 * rank, qw // 2), BF16),
            pltpu.VMEM((2 * rank, kw), BF16),
            pltpu.VMEM((n, 2 * rank, kw), BF16),
            pltpu.VMEM((3, rank, room), F32),
            pltpu.VMEM((3, rank, room), F32),
            pltpu.VMEM((rank, lanes), F32),
            pltpu.VMEM((rank, lanes), F32),
            pltpu.VMEM((2 * rank, lanes), BF16),
            pltpu.VMEM((npair, 2 * rank, lanes), BF16),
            pltpu.VMEM((rank, lanes), F32),
            pltpu.VMEM((n, rank, lanes), F32),
            pltpu.VMEM((width, q_width), BF16),
            pltpu.VMEM((width, kv_width), BF16),
            pltpu.VMEM((width, kv_width), BF16),
            pltpu.SMEM(args[4].shape, jnp.int32),
            pltpu.VMEM(args[5].shape, jnp.int32),
            pltpu.VMEM(hidden.shape, BF16),
            pltpu.VMEM(hidden.shape, BF16),
            pltpu.VMEM(rotation.shape, F32),
            pltpu.VMEM(rotation.shape, F32),
            pltpu.SMEM((rank,), F32),
            dma((len(args),)),
            dma((hist, 2, 2)), dma((hist, 2, 2)),
            dma((4,)), dma((4,)),
            dma, dma,
            dma((npair,)), dma((npair,)),
            dma((n,)), dma((n,)),
            dma((n,)), dma((n,)),
            dma, dma,
            dma, dma,
            dma((npair,)), dma((npair,)),
            dma((n,)), dma((n,)),
        ],
        compiler_params=pltpu.CompilerParams(
            collective_id=0, has_side_effects=True, vmem_limit_bytes=64 << 20
        ),
        name="rank_backward",
    )(*args)
    return pl.pallas_call(
        finish,
        out_shape=tuple(jax.ShapeDtypeStruct(out.shape, out.dtype) for out in outs),
        in_specs=[vmem] * 3,
        out_specs=(vmem,) * 3,
        name="finish",
    )(*outs)


def solution(mesh):
    in_specs = (
        P(("groups", "ctx"), "head"),
        P(("groups", "ctx"), "head"),
        P(("groups", "ctx"), "head"),
        P(("groups", "ctx"), "head"),
        P("groups"),
        P("groups"),
        P("groups", "ctx"),
        P("groups", "ctx"),
        P("ctx", "head"),
        P("ctx", "head"),
        P("ctx", "head"),
        P(None, "ctx"),
        P(None, "ctx"),
        P(),
    )
    out_specs = (P("groups", "ctx"), P("groups", "ctx"), P("groups"))
    return jax.shard_map(
        functools.partial(local, mesh.shape["ctx"]),
        mesh=mesh, in_specs=in_specs, out_specs=out_specs, check_vma=False,
    )
```

```python
import functools

import jax
import jax.numpy as jnp
from jax import lax
from jax.experimental import pallas as pl
from jax.experimental.pallas import tpu as pltpu
from jax.sharding import PartitionSpec as P

HD = 128
BLK = 64
POS_DEV = 8
LANES = 128

scale_q = 1.0 / 12.0
soft_cap = 50.0

MESH = pl.DeviceIdType.MESH
F32 = jnp.float32
BF16 = jnp.bfloat16


def round_up(value, multiple):
    return (value + multiple - 1) // multiple * multiple


def dot(left, right):
    return jnp.dot(left, right, preferred_element_type=F32)


def dot_nt(left, right):
    return lax.dot_general(left, right, (((1,), (1,)), ((), ())), preferred_element_type=F32)


def dot_tn(left, right):
    return lax.dot_general(left, right, (((0,), (0,)), ((), ())), preferred_element_type=F32)


def split2(x):
    hi = x.astype(BF16)
    return hi, (x - hi.astype(F32)).astype(BF16)


def split3(x):
    hi = x.astype(BF16)
    rest = x - hi.astype(F32)
    mid = rest.astype(BF16)
    low = (rest - mid.astype(F32)).astype(BF16)
    return jnp.concatenate([hi, mid, low], axis=0)


def join3(x):
    r = x.shape[0] // 3
    return x[:r] + x[r : 2 * r] + x[2 * r :]


def kernel(
    n,
    q_hbm, k_hbm, v_hbm, g_hbm, doc_hbm, pos_hbm, hidden_hbm, up_hbm,
    wq_hbm, wk_hbm, wv_hbm, rot_hbm, proj_hbm, bias_hbm,
    rot_out, proj_out, bias_out,
    kv, qb, gb, qp, gp, pp, zs, num, zp, nump, ms, sides, kp, vp, rows_all,
    ax_out, ax_own, ax_in, az_out, az_all, tq_out, tq_all, t_out, t_all, sw_out, sw_in,
    st_out, st_in, sz_out, sz_all,
    wq, wk, wv, doc_ref, pos_ref, hidden_ref, up_ref, rot_ref, proj_ref, bias_ref,
    l_sem, z_send, z_recv, x_send, x_recv, xa_send, xa_recv, az_send, az_recv,
    tq_send, tq_recv, t_send, t_recv, sw_send, sw_recv,
    st_send, st_recv, sz_send, sz_recv,
):
    me = lax.axis_index("ctx")
    core = lax.axis_index("head")
    pair = me // 2
    x = lax.rem(me, 2)
    partner = me + 1 - 2 * x
    npair = n // 2
    hist = npair // 2
    tokens = q_hbm.shape[0]
    span = 2 * tokens
    kw = kv.shape[3]
    qw = qb.shape[1]
    kheads = kw // HD
    npos = n * POS_DEV
    mine = 2 * POS_DEV
    lanes = round_up(npos, LANES)
    wide = qw + 2 * kw
    fold = wide // 2

    barrier = pltpu.get_barrier_semaphore()
    for k in range(1, n):
        pl.semaphore_signal(
            barrier, inc=1, device_id={"ctx": lax.rem(me + k, n)}, device_id_type=MESH
        )
    pl.semaphore_signal(barrier, inc=1, device_id={"head": 1 - core}, device_id_type=MESH)

    own_rows = pl.ds(pl.multiple_of(x * tokens, tokens), tokens)

    def cols(ref, which, width):
        return ref.at[:, pl.ds(pl.multiple_of(which * width, width), width)]

    pairs_in = (
        (cols(k_hbm, x, kw), kv.at[0, 0, own_rows]), (cols(v_hbm, x, kw), kv.at[0, 1, own_rows]),
        (doc_hbm, doc_ref), (pos_hbm, pos_ref),
        (cols(q_hbm, x, qw), qb.at[own_rows]), (cols(g_hbm, x, qw), gb.at[own_rows]),
        (rot_hbm, rot_ref), (proj_hbm, proj_ref), (hidden_hbm, hidden_ref),
        (wq_hbm, wq), (wk_hbm, wk), (wv_hbm, wv), (up_hbm, up_ref), (bias_hbm, bias_ref),
    )
    loads = [
        pltpu.make_async_copy(src, dst, l_sem.at[i]) for i, (src, dst) in enumerate(pairs_in)
    ]
    for load in loads:
        load.start()

    def send(src, dst, send_sem, recv_sem, **where):
        return pltpu.make_async_remote_copy(
            src_ref=src, dst_ref=dst, send_sem=send_sem, recv_sem=recv_sem,
            device_id=where, device_id_type=MESH,
        )

    above = lax.rem(me + 2, n)

    def z_copy(j, c, t, run, first=False):
        def go(start, size):
            rows = pl.ds(start, size)
            src = kv.at[j - 1, c, rows]
            if first:
                src = cols((k_hbm, v_hbm)[c], x, kw)
                if size < tokens:
                    src = src.at[pl.ds(tokens - size, size)]
            run(send(src, kv.at[j, c, rows], z_send.at[j - 1, c, t], z_recv.at[j - 1, c, t],
                     ctx=above))
        if j < hist:
            go(pl.multiple_of(t * tokens, tokens), tokens)
        else:
            @pl.when(t == 0)
            def _():
                go(BLK, tokens - BLK)

            @pl.when(t == 1)
            def _():
                go(tokens, tokens)

    def start(copy):
        copy.start()

    def has(j):
        return pair >= j

    def sends(j):
        return jnp.logical_and(pair >= j - 1, pair + 1 < npair)

    other = 1 - x
    x_copies = [
        send(cols(k_hbm, other, kw), kv.at[0, 0, own_rows], x_send.at[0], x_recv.at[0], ctx=partner),
        send(cols(v_hbm, other, kw), kv.at[0, 1, own_rows], x_send.at[1], x_recv.at[1], ctx=partner),
        send(cols(q_hbm, other, qw), qb.at[own_rows], x_send.at[2], x_recv.at[2], ctx=partner),
        send(cols(g_hbm, other, qw), gb.at[own_rows], x_send.at[3], x_recv.at[3], ctx=partner),
    ]

    pl.semaphore_wait(barrier, n)
    for copy in x_copies[:2]:
        copy.start()

    @pl.when(sends(1))
    def _():
        for c in range(2):
            z_copy(1, c, x, start, first=True)

    for load in loads[2:9]:
        load.wait()
    rot = rot_ref[...]
    rank = rot.shape[0]
    rot3 = split3(rot)
    hidden = hidden_ref[...]
    if lanes > npos:
        st_out[...] = jnp.zeros(st_out.shape, F32)
    st_out[:, :npos] = join3(dot_nt(split3(proj_ref[...] - rot), hidden))
    st_copy = send(st_out, st_in, st_send, st_recv, ctx=partner)
    st_copy.start()
    x_copies[2].start()
    for load in loads[9:13]:
        load.wait()
    up = up_ref[...]
    both = []
    for half in range(2):
        both.append(jnp.concatenate([
            join3(dot(rot3, wq[:, half * qw : (half + 1) * qw])),
            join3(dot(rot3, wk[:, half * kw : (half + 1) * kw])),
            join3(dot(rot3, wv[:, half * kw : (half + 1) * kw])),
        ], axis=1))

    def packed(product):
        return jnp.concatenate([product[:, :fold], product[:, fold:]], axis=0)

    ax_out[...] = packed(jnp.where(x == 0, both[1], both[0]))
    xa_copy = send(ax_out, ax_in, xa_send, xa_recv, ctx=partner)
    xa_copy.start()
    x_copies[3].start()
    ax_own[...] = packed(jnp.where(x == 0, both[0], both[1]))

    for c in range(2):
        x_copies[c].wait_recv()

        @pl.when(sends(1))
        def _(c=c):
            z_copy(1, c, other, start)

    def to_pairs(src, dst, send_sem, recv_sem):
        def copy(k, receive):
            slot = lax.rem(pair - k + npair, npair) if receive else pair
            return send(
                src, dst.at[slot], send_sem.at[k - 1], recv_sem.at[slot],
                ctx=lax.rem(me + 2 * k, n),
            )
        return copy

    st_copy.wait_recv()
    sz_out[...] = jnp.concatenate(split2(st_out[...] + st_in[...]), axis=0)
    sz_copy = to_pairs(sz_out, sz_all, sz_send, sz_recv)
    for k in range(1, npair):
        sz_copy(k, False).start()
    sz_all[pair] = sz_out[...]

    blocks = span // BLK
    docs = [doc_ref[pair * blocks + b] for b in range(blocks)]

    def count(i, carry):
        one = doc_ref[i]
        return tuple(s + jnp.where(one < d, BLK, 0) for s, d in zip(carry, docs))

    starts = lax.fori_loop(0, doc_ref.shape[0], count, (jnp.int32(0),) * blocks)
    starts = [s - pair * span for s in starts]

    def start_of(position):
        out = jnp.zeros(position.shape, jnp.int32) + starts[0]
        for b in range(1, blocks):
            out = jnp.where(position >= b * BLK, starts[b], out)
        return out

    row = lax.broadcasted_iota(jnp.int32, (span, span), 0)
    key = lax.broadcasted_iota(jnp.int32, (span, span), 1)
    row_start = start_of(row)
    lane_pos = lax.broadcasted_iota(jnp.int32, (1, npos), 1)
    pick_rel = lane_pos // POS_DEV * tokens + pos_ref[...] - pair * span
    token = lax.broadcasted_iota(jnp.int32, (span, npos), 0)

    def one_hot(j):
        return jnp.where(token - j * span == pick_rel, 1.0, 0.0).astype(BF16)

    hot = one_hot(0)
    my_picks = pl.ds(pl.multiple_of(pair * mine, mine), mine)
    pp[...] = dot_tn(hot, lax.broadcasted_iota(jnp.int32, (span, LANES), 0).astype(F32).astype(BF16))
    where_pick = pp[my_picks, :1].astype(jnp.int32)
    where_pick = jnp.concatenate([where_pick, where_pick], axis=0)
    pick_start = start_of(where_pick)

    if hist > 1:
        for c in range(2):
            @pl.when(has(1))
            def _(c=c):
                z_copy(1, c, x, lambda copy: copy.wait_recv())

            @pl.when(jnp.logical_and(has(1), sends(2)))
            def _(c=c):
                z_copy(2, c, x, start)

    for load in loads[:2]:
        load.wait()
    kv[hist, :, :BLK] = jnp.zeros((2, BLK, kw), BF16)
    kp[...] = dot_tn(hot, kv[0, 0])
    vp[...] = dot_tn(hot, kv[0, 1])

    def visit_rows(j):
        rows = span - BLK if j == hist else span
        seen = key[:rows] - j * span >= row_start[:rows]
        if j == 0:
            seen = seen & (key <= row)
        for h in range(2 * kheads):
            at = slice(h // 2 * HD, (h // 2 + 1) * HD)
            keys, values = kv[j, 0, :, at], kv[j, 1, :, at]
            bent = jnp.tanh(
                dot_nt(qb[:rows, h * HD : (h + 1) * HD], keys) * (scale_q / soft_cap)
            )
            weights = jnp.where(seen, jnp.exp(soft_cap * bent), 0.0)
            folded = weights[:, :LANES]
            for a in range(LANES, span, LANES):
                folded = folded + weights[:, a : a + LANES]
            num_new = dot(weights.astype(BF16), values)
            if j == 0:
                zs[h], num[h] = folded, num_new
            else:
                zs[h, :rows] += folded
                num[h, :rows] += num_new

    def visit_picks(j):
        key_at = key[: 2 * mine] - j * span
        seen = (key_at >= pick_start) & (key_at <= where_pick)
        if j > 0:
            hot_j = one_hot(j)
            kp[...] += dot_tn(hot_j, kv[j, 0])
            vp[...] += dot_tn(hot_j, kv[j, 1])
        for h in range(kheads):
            at = slice(h * HD, (h + 1) * HD)
            keys, values = kv[j, 0, :, at], kv[j, 1, :, at]
            bent = jnp.tanh(dot_nt(qp[h], keys) * (scale_q / soft_cap))
            weights = jnp.where(seen, jnp.exp(soft_cap * bent), 0.0)
            folded = weights[:, :LANES]
            for a in range(LANES, span, LANES):
                folded = folded + weights[:, a : a + LANES]
            num_new = dot(weights.astype(BF16), values)
            side = weights * (1.0 - bent * bent)
            sides[h, j] = side
            ms_new = dot(side.astype(BF16), keys)
            if j == 0:
                zp[h], nump[h], ms[h, 2 * mine :] = folded, num_new, ms_new
            else:
                zp[h] += folded
                nump[h] += num_new
                ms[h, 2 * mine :] += ms_new

    def visit_main(j):
        for h in range(kheads):
            at = slice(h * HD, (h + 1) * HD)
            main = (sides[h, j] * dot_nt(gp[h], kv[j, 1, :, at])).astype(BF16)
            ms_new = dot(main, kv[j, 0, :, at])
            if j == 0:
                ms[h, : 2 * mine] = ms_new
            else:
                ms[h, : 2 * mine] += ms_new

    def arrive(j):
        for t in (x, other):
            if j == 1 and hist > 1 and t is x:
                continue
            for c in range(2):
                z_copy(j, c, t, lambda copy: copy.wait_recv())
                if j < hist:
                    @pl.when(sends(j + 1))
                    def _(c=c, t=t):
                        z_copy(j + 1, c, t, start)

    @pl.when(has(1))
    def _():
        arrive(1)

    def pick_rows(picked, src):
        rows_all[:, :qw] = dot_tn(hot, src[...])
        got = rows_all[my_picks, :qw].astype(BF16)
        for h in range(kheads):
            a, b, c = 2 * h * HD, (2 * h + 1) * HD, (2 * h + 2) * HD
            picked[h] = jnp.concatenate([got[:, a:b], got[:, b:c]], axis=0)

    x_copies[2].wait_recv()
    pick_rows(qp, qb)
    xa_copy.wait_recv()
    az_out[...] = (ax_own[...] + ax_in[...]).astype(BF16)
    az_copy = to_pairs(az_out, az_all, az_send, az_recv)
    for k in range(1, npair):
        az_copy(k, False).start()
    az_all[pair] = jnp.zeros(az_out.shape, BF16)
    ax_own[...] += ax_in[...]

    visit_rows(0)

    @pl.when(has(1))
    def _():
        visit_rows(1)

    visit_picks(0)

    @pl.when(has(1))
    def _():
        visit_picks(1)

    x_copies[3].wait_recv()
    pick_rows(gp, gb)
    visit_main(0)

    @pl.when(has(1))
    def _():
        visit_main(1)

    for j in range(2, hist + 1):
        @pl.when(has(j))
        def _(j=j):
            arrive(j)
            visit_rows(j)
            visit_picks(j)
            visit_main(j)

    rows_all[:, :qw] = jnp.zeros((npos, qw), F32)
    for h in range(kheads):
        at = slice(h * HD, (h + 1) * HD)
        total = jnp.sum(zp[h], axis=1, keepdims=True)
        delta = jnp.sum(gp[h].astype(F32) * (nump[h] / total), axis=1, keepdims=True)
        main, side = ms[h, : 2 * mine], ms[h, 2 * mine :]
        dq = (scale_q * (main - delta * side) / total).astype(BF16).astype(F32)
        for i in range(2):
            rows_all[my_picks, (2 * h + i) * HD : (2 * h + i + 1) * HD] = dq[
                i * mine : (i + 1) * mine
            ]

    for k in range(1, npair):
        sz_copy(k, True).wait_recv()
    sz = sz_all[0].astype(F32)
    for i in range(1, npair):
        sz = sz + sz_all[i].astype(F32)
    rank_state = sz[:rank, :npos] + sz[rank:, :npos]
    loads[13].wait()
    bias_row = lax.broadcasted_iota(jnp.int32, rank_state.shape, 0)
    for r in range(rank):
        rank_state = rank_state + jnp.where(bias_row == r, bias_ref[r], 0.0)

    s_hi, s_lo = split2(rank_state)
    s_both = jnp.concatenate([s_hi, s_lo], axis=0)
    q_rows = rows_all[:, :qw].astype(BF16)
    q2 = dot(s_both, q_rows)
    term = q2[:rank] + q2[rank:]
    tq_out[...] = jnp.concatenate([term[:, : qw // 2], term[:, qw // 2 :]], axis=0).astype(BF16)

    def to_all(src, dst, send_sem, recv_sem):
        def each(run):
            for d in range(n):
                @pl.when(me != d)
                def _(d=d):
                    run(d)

        def begin():
            each(lambda d: send(
                src, dst.at[me], send_sem.at[d], recv_sem.at[me], ctx=d
            ).start())

        def received():
            each(lambda d: send(
                src, dst.at[d], send_sem.at[d], recv_sem.at[d], ctx=d
            ).wait_recv())

        def gone():
            each(lambda d: send(
                src, dst.at[me], send_sem.at[d], recv_sem.at[me], ctx=d
            ).wait_send())

        return begin, received, gone

    tq_begin, tq_received, tq_gone = to_all(tq_out, tq_all, tq_send, tq_recv)
    tq_begin()
    tq_all[me] = tq_out[...]

    row1 = lax.broadcasted_iota(jnp.int32, (span, npos), 0)
    seen = (pick_rel >= start_of(row1)) & (pick_rel <= row1)
    for h in range(kheads):
        at = slice(h * HD, (h + 1) * HD)
        keys = kp[:, at].astype(BF16)
        values = vp[:, at].astype(BF16)
        dk = dv = 0.0
        for i in range(2 * h, 2 * h + 2):
            query = qb[:, i * HD : (i + 1) * HD]
            grad = gb[:, i * HD : (i + 1) * HD]
            total = jnp.sum(zs[i], axis=1, keepdims=True)
            delta = jnp.sum(grad.astype(F32) * (num[i] / total), axis=1, keepdims=True)
            bent = jnp.tanh(dot_nt(query, keys) * (scale_q / soft_cap))
            prob = jnp.where(seen, jnp.exp(soft_cap * bent), 0.0) / total
            dscore = prob * (dot_nt(grad, values) - delta) * (1.0 - bent * bent)
            dv = dv + dot_tn(prob.astype(BF16), grad)
            dk = dk + dot_tn(dscore.astype(BF16), query)
        rows_all[:, qw + h * HD : qw + (h + 1) * HD] = scale_q * dk
        rows_all[:, qw + kw + h * HD : qw + kw + (h + 1) * HD] = dv

    r_hi, r_lo = split2(rows_all[:, qw:])
    k2 = dot(s_both, r_hi)
    term = k2[:rank] + k2[rank:] + dot(s_hi, r_lo)
    rank_up = join3(dot_nt(rot3, up))
    first_core = jnp.where(core == 0, 1.0, 0.0)
    for k in range(1, npair):
        az_copy(k, True).wait_recv()
    az = ax_own[...] + az_all[0].astype(F32)
    for i in range(1, npair):
        az = az + az_all[i].astype(F32)
    rw = jnp.concatenate([az[:rank], az[rank:]], axis=1)
    a_hi, a_lo = split2(rw)
    a_both = jnp.concatenate([a_hi, a_lo], axis=0)
    a2 = dot_nt(a_both[:, :qw], q_rows) + dot_nt(a_both[:, qw:], r_hi)
    rg = a2[:rank] + a2[rank:] + dot_nt(a_hi[:, qw:], r_lo) + first_core * rank_up
    if lanes > npos:
        t_out[:, kw:] = jnp.zeros((2 * rank, lanes), BF16)
    t_out[:, :kw] = jnp.concatenate([term[:, :kw], term[:, kw:]], axis=0).astype(BF16)
    t_out[:, kw : kw + npos] = jnp.concatenate(split2(rg), axis=0)
    t_begin, t_received, t_gone = to_all(t_out, t_all, t_send, t_recv)
    t_begin()
    t_all[me] = t_out[...]
    rot_up = first_core * join3(dot(split3(rank_state), up))

    def sum_over_pairs(ref):
        sums = []
        for i in range(2):
            total = ref[i].astype(F32)
            for z in range(1, npair):
                total = total + ref[2 * z + i].astype(F32)
            sums.append(total)
        return sums

    def weighted(w, parts):
        return dot_nt(w[...], jnp.concatenate(split2(jnp.concatenate(parts, axis=1)), axis=0))

    tq_received()
    res = weighted(
        wq, [p for s in sum_over_pairs(tq_all) for p in (s[:rank], s[rank:])]
    )
    t_received()
    sums = sum_over_pairs(t_all)
    res = res + weighted(wk, [s[:rank, :kw] for s in sums])
    res = res + weighted(wv, [s[rank:, :kw] for s in sums])
    res = jnp.transpose(res)
    grad = res[:rank] + res[rank:] + rot_up
    rg = sums[0][:, kw : kw + npos] + sums[1][:, kw : kw + npos]
    rg = rg[:rank] + rg[rank:]
    grad_proj = join3(dot(split3(rg), hidden))

    width = hidden.shape[1]
    room = sw_out.shape[2]
    if room > width:
        sw_out[0] = jnp.zeros((rank, room), F32)
        sw_out[1] = jnp.zeros((rank, room), F32)
    sw_out[0, :, :width] = grad - grad_proj
    sw_out[1, :, :width] = grad_proj
    sw_out[2, :, :lanes] = jnp.broadcast_to(jnp.sum(rg, axis=1, keepdims=True), (rank, lanes))
    sw_copy = send(sw_out, sw_in, sw_send, sw_recv, head=1 - core)
    sw_copy.start()
    sw_copy.wait_recv()
    rot_out[...] = sw_out[0, :, :width] + sw_in[0, :, :width]
    proj_out[...] = sw_out[1, :, :width] + sw_in[1, :, :width]
    bias = sw_out[2, :, :lanes] + sw_in[2, :, :lanes]
    for r in range(rank):
        bias_out[r] = bias[r, 0]

    sw_copy.wait_send()
    xa_copy.wait_send()
    for copy in x_copies:
        copy.wait_send()
    for k in range(1, npair):
        az_copy(k, False).wait_send()
        sz_copy(k, False).wait_send()
    st_copy.wait_send()
    tq_gone()
    t_gone()

    def sent(copy):
        copy.wait_send()

    for j in range(1, hist + 1):
        @pl.when(sends(j))
        def _(j=j):
            for c in range(2):
                z_copy(j, c, x, sent, first=j == 1)
                z_copy(j, c, other, sent)


def finish(rot_in, proj_in, bias_in, rot_out, proj_out, bias_out):
    rot_out[...] = rot_in[...]
    proj_out[...] = proj_in[...]
    bias_out[...] = bias_in[...]


def local(n, *args):
    args = list(args)
    args[5] = args[5].reshape(1, -1)
    queries, key_states = args[0], args[1]
    hidden, rotation = args[6], args[11]
    tokens, q_width = queries.shape
    kv_width = key_states.shape[1]
    qw, kw = q_width // 2, kv_width // 2
    kheads = kw // HD
    width = hidden.shape[1]
    rank = rotation.shape[0]
    npair = n // 2
    hist = npair // 2
    npos = n * POS_DEV
    mine = 2 * POS_DEV
    lanes = round_up(npos, LANES)
    span = 2 * tokens
    wide = qw + 2 * kw
    fold = wide // 2
    room = max(round_up(width, LANES), lanes)
    vmem = pl.BlockSpec(memory_space=pltpu.VMEM)
    smem = pl.BlockSpec(memory_space=pltpu.SMEM)
    hbm = pl.BlockSpec(memory_space=pltpu.HBM)
    dma = pltpu.SemaphoreType.DMA
    outs = pl.pallas_call(
        functools.partial(kernel, n),
        out_shape=(
            jax.ShapeDtypeStruct((rank, width), F32),
            jax.ShapeDtypeStruct((rank, width), F32),
            jax.ShapeDtypeStruct((rank,), F32),
        ),
        in_specs=[hbm] * len(args),
        out_specs=(vmem, vmem, smem),
        scratch_shapes=[
            pltpu.VMEM((hist + 1, 2, span, kw), BF16),
            pltpu.VMEM((span, qw), BF16),
            pltpu.VMEM((span, qw), BF16),
            pltpu.VMEM((kheads, 2 * mine, HD), BF16),
            pltpu.VMEM((kheads, 2 * mine, HD), BF16),
            pltpu.VMEM((npos, LANES), F32),
            pltpu.VMEM((2 * kheads, span, LANES), F32),
            pltpu.VMEM((2 * kheads, span, HD), F32),
            pltpu.VMEM((kheads, 2 * mine, LANES), F32),
            pltpu.VMEM((kheads, 2 * mine, HD), F32),
            pltpu.VMEM((kheads, 4 * mine, HD), F32),
            pltpu.VMEM((kheads, hist + 1, 2 * mine, span), F32),
            pltpu.VMEM((npos, kw), F32),
            pltpu.VMEM((npos, kw), F32),
            pltpu.VMEM((npos, wide), F32),
            pltpu.VMEM((2 * rank, fold), F32),
            pltpu.VMEM((2 * rank, fold), F32),
            pltpu.VMEM((2 * rank, fold), F32),
            pltpu.VMEM((2 * rank, fold), BF16),
            pltpu.VMEM((npair, 2 * rank, fold), BF16),
            pltpu.VMEM((2 * rank, qw // 2), BF16),
            pltpu.VMEM((n, 2 * rank, qw // 2), BF16),
            pltpu.VMEM((2 * rank, kw + lanes), BF16),
            pltpu.VMEM((n, 2 * rank, kw + lanes), BF16),
            pltpu.VMEM((3, rank, room), F32),
            pltpu.VMEM((3, rank, room), F32),
            pltpu.VMEM((rank, lanes), F32),
            pltpu.VMEM((rank, lanes), F32),
            pltpu.VMEM((2 * rank, lanes), BF16),
            pltpu.VMEM((npair, 2 * rank, lanes), BF16),
            pltpu.VMEM((width, q_width), BF16),
            pltpu.VMEM((width, kv_width), BF16),
            pltpu.VMEM((width, kv_width), BF16),
            pltpu.SMEM(args[4].shape, jnp.int32),
            pltpu.VMEM(args[5].shape, jnp.int32),
            pltpu.VMEM(hidden.shape, BF16),
            pltpu.VMEM(hidden.shape, BF16),
            pltpu.VMEM(rotation.shape, F32),
            pltpu.VMEM(rotation.shape, F32),
            pltpu.SMEM((rank,), F32),
            dma((len(args),)),
            dma((hist, 2, 2)), dma((hist, 2, 2)),
            dma((4,)), dma((4,)),
            dma, dma,
            dma((npair,)), dma((npair,)),
            dma((n,)), dma((n,)),
            dma((n,)), dma((n,)),
            dma, dma,
            dma, dma,
            dma((npair,)), dma((npair,)),
        ],
        compiler_params=pltpu.CompilerParams(
            collective_id=0, has_side_effects=True, vmem_limit_bytes=64 << 20
        ),
        name="rank_backward",
    )(*args)
    return pl.pallas_call(
        finish,
        out_shape=tuple(jax.ShapeDtypeStruct(out.shape, out.dtype) for out in outs),
        in_specs=[vmem] * 3,
        out_specs=(vmem,) * 3,
        name="finish",
    )(*outs)


def solution(mesh):
    in_specs = (
        P(("groups", "ctx"), "head"),
        P(("groups", "ctx"), "head"),
        P(("groups", "ctx"), "head"),
        P(("groups", "ctx"), "head"),
        P("groups"),
        P("groups"),
        P("groups", "ctx"),
        P("groups", "ctx"),
        P("ctx", "head"),
        P("ctx", "head"),
        P("ctx", "head"),
        P(None, "ctx"),
        P(None, "ctx"),
        P(),
    )
    out_specs = (P("groups", "ctx"), P("groups", "ctx"), P("groups"))
    return jax.shard_map(
        functools.partial(local, mesh.shape["ctx"]),
        mesh=mesh, in_specs=in_specs, out_specs=out_specs, check_vma=False,
    )
```
